256 devices in a mesh: ctx: 32 (over z, y), head: 8 (over x, core).
Axes of the slice: x: 4, y: 4, z: 8, core: 2. Of those that a mesh axis runs over, the one named last changes fastest.
Arguments:
- query: bfloat16 [8192, 8192], P(('ctx', 'head')), may hold values from -64 to 64
- key: bfloat16 [8192, 1024], P(('ctx', 'head')), may hold values from -6 to 6
- value: bfloat16 [8192, 1024], P(('ctx', 'head')), may hold values from -6 to 6
- grad_out: bfloat16 [8192, 8192], P('ctx', 'head'), may hold values from -6 to 6
- doc_ids: int32 [64], replicated, may hold values from 0 to 5, never falling along the last dimension, each value on 1 to 16 neighbouring positions
- relay_mask: int32 [2], replicated, may hold values from 0 to 31
- drop_bits: int32 [64, 128, 4], P('head'), may hold values from -2147483648 to 2147483647
Outputs:
- out: bfloat16 [8192, 8192], P('ctx', 'head')
- grad_query: bfloat16 [8192, 8192], P(('ctx', 'head'))
- grad_key: bfloat16 [8192, 1024], P(('ctx', 'head'))
- grad_value: bfloat16 [8192, 1024], P(('ctx', 'head'))
The draws below stay inside these ranges and needn't reach their ends.
Inputs may be any that keep to these rules, and one draw needn't show every extreme that they name: `doc_ids`: numbers never fall; each document spans 1 to 16 blocks and one spans exactly 16.
All inputs are finite; a program needn't handle non-finite values.
Results may differ from the reference program's by a relative error of at most 0.033.
Values may be sent and summed in bfloat16 or wider, within the bound.
A program may use at most 64 MiB of HBM per device.

```python
import math
import jax
import jax.numpy as jnp
import numpy as np
from jax import lax

E = 128
BLK = 128
BLK_DEV = 2
HEADS = 64
KVH = 8
SEQ = 8192
NBLK = 64
MAXDOC = 16
DOCS = 6
N_CTX = 32


def key_matrix(key):
    base_draw = jnp.clip(jax.random.normal(jax.random.fold_in(key, 11), (SEQ, KVH * E), jnp.float32), -6.0, 6.0)
    return base_draw


def draw_key(key, part):
    base_draw = key_matrix(key)
    return base_draw.astype(jnp.bfloat16)


def draw_query(key, part):
    base_draw = jnp.clip(jax.random.normal(jax.random.fold_in(key, 21), (SEQ, HEADS * E), jnp.float32), -6.0, 6.0)
    return base_draw.astype(jnp.bfloat16)


def draw_drop_bits(key, part):
    digits = jax.random.randint(key, (HEADS, BLK, BLK // 32, 32), 0, 10, dtype=jnp.int32)
    bit_values = (digits < 9).astype(jnp.int32)
    shifted = jnp.left_shift(bit_values, jnp.arange(32, dtype=jnp.int32))
    return jnp.sum(shifted, axis=-1).astype(jnp.int32)


def block_scale(key, dims, split, smallest, high):
    level, own = 1.0, jax.random.fold_in(key, 6)
    for position, shards_of in split:
        heights = jnp.exp(jax.random.uniform(jax.random.fold_in(own, position), (shards_of,), jnp.float32, smallest / len(split), high / len(split)))
        level = level * jnp.repeat(heights, dims[position] // shards_of).reshape([-1 if axis == position else 1 for axis in range(len(dims))])
    return level


def split_up(count, total, reach, slope):
    portions = [(1 << 20) // math.isqrt(standing ** slope) + 1 for standing in range(2, count + 1)]
    surplus, counts = total - reach - (count - 1), [1] * (count - 1)
    while surplus > 0:
        movable = [i for i in range(count - 1) if counts[i] < reach]
        whole, left = sum([portions[i] for i in movable]), surplus
        for i in movable:
            extra = min(reach - counts[i], max(1, left * portions[i] // whole), surplus)
            counts[i] = counts[i] + extra
            surplus = surplus - extra
    return np.array([reach] + counts)


def ragged(key, count, total, reach, lean):
    if count == 2:
        one = jax.random.randint(key, (), max(1, total - reach), min(reach, total - 1) + 1)
        return jnp.stack([one, total - one])
    lengths = jnp.asarray(split_up(count, total, reach, lean), jnp.int32)
    couples = (count - 1) // 2
    donor, taker = lengths[1:1 + 2 * couples:2], lengths[2:2 + 2 * couples:2]
    margin = jnp.minimum(donor - 1, reach - taker)
    passed = jax.random.randint(jax.random.fold_in(key, 1), (couples,), 0, 1 << 20) % (margin + 1)
    lengths = lengths.at[1:1 + 2 * couples:2].set(donor - passed).at[2:2 + 2 * couples:2].set(taker + passed)
    return lengths[jax.random.permutation(jax.random.fold_in(key, 2), count)]


def noise(stream_key, extent, deviation, limit, pieces=(), kind=jnp.bfloat16):
    values = jax.random.normal(stream_key, extent, jnp.float32) * deviation
    if len(pieces) > 0:
        values = block_scale(stream_key, extent, pieces, -0.22, 0.18) * values
    return jnp.clip(values, min=-limit, max=limit).astype(kind)


def setup_inputs(seed: int = 0) -> dict:
    key_of = jax.random.split(jax.random.key(seed), 8)
    return {
        "query": draw_query(jax.random.fold_in(key_of[7], 71), 0),
        "key": draw_key(jax.random.fold_in(key_of[7], 71), 0),
        "value": noise(key_of[2], (SEQ, KVH * E), 1.0, 6.0, ((0, 256),)),
        "grad_out": noise(key_of[3], (SEQ, HEADS * E), 1.0, 6.0, ((0, 32), (1, 8))),
        "doc_ids": jnp.searchsorted(jnp.cumsum(ragged(key_of[4], DOCS, NBLK, MAXDOC, 1)), jnp.arange(NBLK), side="right").astype(jnp.int32),
        "relay_mask": jax.random.randint(key_of[5], (BLK_DEV,), 0, N_CTX).astype(jnp.int32),
        "drop_bits": draw_drop_bits(jax.random.fold_in(key_of[7], 71), 0),
    }


drop_scale = 1.0 / 0.9

def unpack_bits(packed_words):
    shifts = jnp.arange(32, dtype=jnp.int32)
    bit_values = jnp.right_shift(packed_words[..., None], shifts) & 1
    return bit_values.reshape(packed_words.shape[:-1] + (packed_words.shape[-1] * 32,)).astype(jnp.float32)

def keep_tile(doubled, block_index):
    start_row = (block_index % BLK).astype(jnp.int32)
    table_rows = lax.dynamic_slice(doubled, (jnp.int32(0), start_row, jnp.int32(0)), (doubled.shape[0], BLK, doubled.shape[2]))
    return unpack_bits(table_rows)

def reference(query, key, value, grad_out, doc_ids, relay_mask, drop_bits):
    inv_root = 1.0 / math.sqrt(E)
    nblocks = SEQ // BLK
    window = MAXDOC * BLK
    group_size = HEADS // KVH
    blocks = jnp.arange(nblocks, dtype=jnp.int32)
    source = BLK_DEV * jnp.bitwise_xor(blocks // BLK_DEV, relay_mask[blocks % BLK_DEV]) + blocks % BLK_DEV
    grads_packed = grad_out.reshape(nblocks, BLK, HEADS * E)[source].reshape(SEQ, KVH, group_size, E)
    queries = query.reshape(SEQ, KVH, group_size, E)
    keys = key.reshape(SEQ, KVH, E)
    values = value.reshape(SEQ, KVH, E)
    doubled = jnp.concatenate([drop_bits, drop_bits], axis=1)

    def terms(query_block):
        first_block = jnp.maximum(query_block - MAXDOC + 1, 0).astype(jnp.int32)
        query_rows = lax.dynamic_slice_in_dim(queries, query_block * BLK, BLK, 0).astype(jnp.float32)
        key_window = lax.dynamic_slice_in_dim(keys, first_block * BLK, window, 0).astype(jnp.float32)
        value_window = lax.dynamic_slice_in_dim(values, first_block * BLK, window, 0).astype(jnp.float32)
        scores = jnp.einsum('qgne,kge->gnqk', query_rows, key_window) * inv_root
        query_pos = query_block * BLK + jnp.arange(BLK, dtype=jnp.int32)
        key_pos = first_block * BLK + jnp.arange(window, dtype=jnp.int32)
        key_docs = doc_ids[key_pos // BLK]
        allowed = (key_docs[None, :] == doc_ids[query_block]) & (key_pos[None, :] <= query_pos[:, None])
        masked = jnp.where(allowed, scores, -jnp.inf)
        row_max = lax.optimization_barrier(jnp.max(masked, axis=-1, keepdims=True))
        log_total = row_max + jnp.log(lax.optimization_barrier(jnp.sum(jnp.exp(masked - row_max), axis=-1, keepdims=True)))
        probabilities = jnp.where(allowed, jnp.exp(scores - log_total), 0.0)
        keep_bits = jax.vmap(lambda offset: keep_tile(doubled, first_block + offset))(jnp.arange(MAXDOC, dtype=jnp.int32))
        keep_bits = keep_bits.transpose(1, 2, 0, 3).reshape(KVH, group_size, BLK, window)
        weights = lax.optimization_barrier((probabilities * keep_bits * drop_scale).astype(jnp.bfloat16))
        return (first_block, query_rows, key_window, value_window, probabilities, keep_bits, weights.astype(jnp.float32))

    def forward(query_block):
        first_block, query_rows, key_window, value_window, probabilities, keep_bits, weights = terms(query_block)
        result = jnp.einsum('gnqk,kge->qgne', weights, value_window)
        return result.reshape(BLK, HEADS * E).astype(jnp.bfloat16)
    out_packed = lax.map(forward, blocks)
    out_bal = out_packed[source].reshape(SEQ, HEADS * E)

    def backward(carried, query_block):
        grad_keys, grad_values = carried
        first_block, query_rows, key_window, value_window, probabilities, keep_bits, weights = terms(query_block)
        grad_rows = lax.dynamic_slice_in_dim(grads_packed, query_block * BLK, BLK, 0).astype(jnp.float32)
        out_rows = out_packed[query_block].reshape(BLK, KVH, group_size, E).astype(jnp.float32)
        row_delta = lax.optimization_barrier(jnp.sum(grad_rows * out_rows, axis=-1)).transpose(1, 2, 0)
        dweights = jnp.einsum('qgne,kge->gnqk', grad_rows, value_window)
        dscores = (probabilities * (dweights * keep_bits * drop_scale - row_delta[..., None])).astype(jnp.bfloat16)
        dscores = lax.optimization_barrier(dscores).astype(jnp.float32)
        query_grad = (inv_root * jnp.einsum('gnqk,kge->qgne', dscores, key_window)).reshape(BLK, HEADS * E).astype(jnp.bfloat16)
        key_grad = inv_root * jnp.einsum('gnqk,qgne->kge', dscores, query_rows)
        value_grad = jnp.einsum('gnqk,qgne->kge', weights, grad_rows)
        start_row = first_block * BLK
        grad_keys = lax.dynamic_update_slice_in_dim(grad_keys, lax.dynamic_slice_in_dim(grad_keys, start_row, window, 0) + key_grad, start_row, 0)
        grad_values = lax.dynamic_update_slice_in_dim(grad_values, lax.dynamic_slice_in_dim(grad_values, start_row, window, 0) + value_grad, start_row, 0)
        return ((grad_keys, grad_values), query_grad)
    initial = (jnp.zeros((SEQ, KVH, E), jnp.float32), jnp.zeros((SEQ, KVH, E), jnp.float32))
    (grad_keys, grad_values), grad_queries = lax.scan(backward, initial, blocks)
    return (out_bal, grad_queries.reshape(SEQ, HEADS * E), grad_keys.reshape(SEQ, KVH * E).astype(jnp.bfloat16), grad_values.reshape(SEQ, KVH * E).astype(jnp.bfloat16))
```

```python
import math

import jax
import jax.numpy as jnp
from jax import lax
from jax.experimental import pallas as pl
from jax.experimental.pallas import tpu as pltpu
from jax.sharding import PartitionSpec as P

E = 128
BLK = 128
GROUP = 8
PAIRS = 8
WIN = 18 * BLK
NZ, NY, NH = 8, 4, 8
F32 = jnp.float32
BF16 = jnp.bfloat16
MESH = pl.DeviceIdType.MESH


def place():
    ctx, head = lax.axis_index("ctx"), lax.axis_index("head")
    return ctx // NY, ctx % NY, head


def remote(src, dst, send, recv, ctx, head):
    return pltpu.make_async_remote_copy(
        src_ref=src, dst_ref=dst, send_sem=send, recv_sem=recv,
        device_id=(ctx, head), device_id_type=MESH)


def greet(zi, yi, head):
    barrier = pltpu.get_barrier_semaphore()
    peers = [(zi * NY + yi, (head + d) % NH) for d in range(1, NH)]
    peers += [(((zi + d) % NZ) * NY + yi, head) for d in (1, 2, NZ - 1, NZ - 2)]
    peers += [(zi * NY + (yi + k) % NY, head) for k in range(1, NY)]
    for peer in peers:
        pl.semaphore_signal(barrier, inc=1, device_id=peer, device_id_type=MESH)
    pl.semaphore_wait(barrier, len(peers))


def gather_kernel(q_ref, k_ref, v_ref, qb_ref, win_ref, kv_send, kv_recv, q_send, q_recv,
                  z_send, z_recv, y_send, y_recv, own_sem):
    zi, yi, head = place()
    ctx = zi * NY + yi
    greet(zi, yi, head)
    mine = pl.ds(pl.multiple_of(head * 32, 32), 32)
    own = [
        pltpu.make_async_copy(k_ref.at[:, pl.ds(pl.multiple_of(head * E, E), E)],
                              win_ref.at[8, mine, pl.ds(0, E)], own_sem.at[0]),
        pltpu.make_async_copy(v_ref.at[:, pl.ds(pl.multiple_of(head * E, E), E)],
                              win_ref.at[8, mine, pl.ds(E, E)], own_sem.at[1]),
        pltpu.make_async_copy(q_ref.at[:, pl.ds(pl.multiple_of(head * GROUP * E, GROUP * E), GROUP * E)],
                              qb_ref.at[mine, :], own_sem.at[2]),
    ]
    for copy in own:
        copy.start()
    kv_copies = []
    for d in range(1, NH):
        to = (head + d) % NH
        cols = pl.ds(pl.multiple_of(to * E, E), E)
        for part, ref in enumerate((k_ref, v_ref)):
            copy = remote(ref.at[:, cols], win_ref.at[8, mine, pl.ds(part * E, E)],
                          kv_send.at[part, d], kv_recv.at[part, d], ctx, to)
            copy.start()
            kv_copies.append(copy)
    q_copies = []
    for d in range(1, NH):
        to = (head + d) % NH
        cols = pl.ds(pl.multiple_of(to * GROUP * E, GROUP * E), GROUP * E)
        copy = remote(q_ref.at[:, cols], qb_ref.at[mine, :], q_send.at[d], q_recv.at[d], ctx, to)
        copy.start()
        q_copies.append(copy)
    own[0].wait()
    own[1].wait()
    for copy in kv_copies:
        copy.wait_recv()
    z_copies = []
    for d in (1, 2):
        copy = remote(win_ref.at[8], win_ref.at[8 - 4 * d], z_send.at[d], z_recv.at[d],
                      ((zi + d) % NZ) * NY + yi, head)
        copy.start()
        z_copies.append(copy)
    y_copies = []
    for part in range(2):
        for k in range(1, NY):
            wrap = (yi + k) // NY
            y_copies.append((part, k, wrap, remote(
                win_ref.at[8 - 4 * part - 4 * wrap], win_ref.at[8 - 4 * part - k],
                y_send.at[part, k], y_recv.at[part, k], zi * NY + (yi + k) % NY, head)))
    for part, k, wrap, copy in y_copies:
        if part == 0:
            @pl.when(wrap == 0)
            def _(copy=copy):
                copy.start()
    z_copies[0].wait_recv()
    for part, k, wrap, copy in y_copies:
        @pl.when(wrap == 1 - part)
        def _(copy=copy):
            copy.start()
    z_copies[1].wait_recv()
    for part, k, wrap, copy in y_copies:
        if part == 1:
            @pl.when(wrap == 1)
            def _(copy=copy):
                copy.start()
    for copy in q_copies:
        copy.wait_recv()
    for _, _, _, copy in y_copies:
        copy.wait_recv()
    own[2].wait()
    for copy in kv_copies + q_copies + z_copies:
        copy.wait_send()
    for _, _, _, copy in y_copies:
        copy.wait_send()


def gather_inputs(query, key, value):
    vm = pl.BlockSpec(memory_space=pltpu.VMEM)
    dma = pltpu.SemaphoreType.DMA
    return pl.pallas_call(
        gather_kernel,
        out_shape=(jax.ShapeDtypeStruct((2 * BLK, GROUP * E), BF16),
                   jax.ShapeDtypeStruct((9, 2 * BLK, 2 * E), BF16)),
        in_specs=[vm, vm, vm],
        out_specs=(vm, vm),
        scratch_shapes=[dma((2, NH)), dma((2, NH)), dma((NH,)), dma((NH,)), dma((3,)), dma((3,)),
                        dma((2, NY)), dma((2, NY)), dma((3,))],
        compiler_params=pltpu.CompilerParams(collective_id=0, has_side_effects=True),
    )(query, key, value)


def scatter_kernel(dkv_ref, dq_ref, gq_ref, gk_ref, gv_ref, r_ref, zs_ref, zr_ref, own_ref, fin_ref,
                   q_send, q_recv, y_send, y_recv, z_send, z_recv, kv_send, kv_recv, own_sem):
    zi, yi, head = place()
    ctx = zi * NY + yi
    greet(zi, yi, head)
    wide = pl.ds(pl.multiple_of(head * GROUP * E, GROUP * E), GROUP * E)
    slim = pl.ds(pl.multiple_of(head * E, E), E)
    y_copies = []
    for part in (1, 0):
        for k in range(1, NY):
            copy = remote(dkv_ref.at[8 - 4 * part - k], r_ref.at[part, k - 1],
                          y_send.at[part, k], y_recv.at[part, k],
                          zi * NY + (yi + NY - k) % NY, head)
            copy.start()
            y_copies.append(copy)
    q_copies = []
    for d in range(1, NH):
        to = (head + d) % NH
        rows = pl.ds(pl.multiple_of(to * 32, 32), 32)
        copy = remote(dq_ref.at[rows, :], gq_ref.at[:, wide], q_send.at[d], q_recv.at[d], ctx, to)
        copy.start()
        q_copies.append(copy)
    mine = pl.ds(pl.multiple_of(head * 32, 32), 32)
    own = [pltpu.make_async_copy(dq_ref.at[mine, :], gq_ref.at[:, wide], own_sem.at[0])]
    own[0].start()
    for copy in y_copies:
        copy.wait_recv()
    sums = [dkv_ref[8 - 4 * p].astype(F32) for p in range(3)]
    for k in range(1, NY):
        wraps = (yi + k) // NY > 0
        first, second = r_ref[0, k - 1].astype(F32), r_ref[1, k - 1].astype(F32)
        zero = jnp.zeros_like(first)
        sums[0] = sums[0] + jnp.where(wraps, zero, first)
        sums[1] = sums[1] + jnp.where(wraps, first, second)
        sums[2] = sums[2] + jnp.where(wraps, second, zero)
    zs_ref[0] = sums[1].astype(BF16)
    zs_ref[1] = sums[2].astype(BF16)
    own_ref[...] = sums[0]
    z_copies = []
    for d in (1, 2):
        copy = remote(zs_ref.at[d - 1], zr_ref.at[d - 1], z_send.at[d], z_recv.at[d],
                      ((zi + NZ - d) % NZ) * NY + yi, head)
        copy.start()
        z_copies.append(copy)
    for copy in z_copies:
        copy.wait_recv()
    fin_ref[...] = (own_ref[...] + zr_ref[0].astype(F32) + zr_ref[1].astype(F32)).astype(BF16)
    kv_copies = []
    for d in range(1, NH):
        to = (head + d) % NH
        rows = pl.ds(pl.multiple_of(to * 32, 32), 32)
        for part, ref in enumerate((gk_ref, gv_ref)):
            copy = remote(fin_ref.at[rows, pl.ds(part * E, E)], ref.at[:, slim],
                          kv_send.at[part, d], kv_recv.at[part, d], ctx, to)
            copy.start()
            kv_copies.append(copy)
    for part, ref in enumerate((gk_ref, gv_ref)):
        copy = pltpu.make_async_copy(fin_ref.at[mine, pl.ds(part * E, E)], ref.at[:, slim],
                                     own_sem.at[1 + part])
        copy.start()
        own.append(copy)
    for copy in q_copies + kv_copies:
        copy.wait_recv()
    for copy in own:
        copy.wait()
    for copy in q_copies + kv_copies + y_copies + z_copies:
        copy.wait_send()


def scatter_grads(dkv, dq):
    vm = pl.BlockSpec(memory_space=pltpu.VMEM)
    dma = pltpu.SemaphoreType.DMA
    return pl.pallas_call(
        scatter_kernel,
        out_shape=(jax.ShapeDtypeStruct((32, NH * GROUP * E), BF16),
                   jax.ShapeDtypeStruct((32, NH * E), BF16),
                   jax.ShapeDtypeStruct((32, NH * E), BF16)),
        in_specs=[vm, vm],
        out_specs=(vm, vm, vm),
        scratch_shapes=[
            pltpu.VMEM((2, NY - 1, 2 * BLK, 2 * E), BF16),
            pltpu.VMEM((2, 2 * BLK, 2 * E), BF16),
            pltpu.VMEM((2, 2 * BLK, 2 * E), BF16),
            pltpu.VMEM((2 * BLK, 2 * E), F32),
            pltpu.VMEM((2 * BLK, 2 * E), BF16),
            dma((NH,)), dma((NH,)), dma((2, NY)), dma((2, NY)), dma((3,)), dma((3,)),
            dma((2, NH)), dma((2, NH)), dma((3,))],
        compiler_params=pltpu.CompilerParams(collective_id=1, has_side_effects=True),
    )(dkv, dq)


def dot_nt(a, b):
    return lax.dot_general(a, b, (((1,), (1,)), ((), ())), preferred_element_type=F32)


def dot_nn(a, b):
    return lax.dot_general(a, b, (((1,), (0,)), ((), ())), preferred_element_type=F32)


def attn_kernel(docs_ref, q_ref, kv_ref, g_ref, bits_ref, out_ref, dq_ref, dkv_ref,
                s_ref, w_ref, keep_ref, qs_ref, gs_ref, qt_ref, gt_ref, acc_ref, mx_ref,
                dkt_ref, dvt_ref, st_ref):
    root = 1.0 / math.sqrt(E)
    expo = root * math.log2(math.e)
    scale = 1.0 / 0.9
    lane = lax.broadcasted_iota(jnp.int32, (BLK, BLK), 1)
    row = lax.broadcasted_iota(jnp.int32, (BLK, BLK), 0)
    shift = lane % 32
    for h in range(GROUP):
        words = bits_ref[h]
        spread = jnp.where(lane < 64,
                           jnp.where(lane < 32, words[:, 0:1], words[:, 1:2]),
                           jnp.where(lane < 96, words[:, 2:3], words[:, 3:4]))
        kept = (lax.shift_right_logical(spread, shift) & 1).astype(F32)
        keep_ref[h, 0:BLK] = kept
        keep_ref[h, BLK:2 * BLK] = kept
    dkt_ref[...] = jnp.zeros_like(dkt_ref)
    dvt_ref[...] = jnp.zeros_like(dvt_ref)
    first_abs = 2 * lax.axis_index("ctx") - 16
    causal = jnp.where(lane <= row, 0.0, -jnp.inf).astype(F32)
    lane2 = lax.broadcasted_iota(jnp.int32, (1, 2 * BLK), 1)

    for r in range(2):
        document = docs_ref[first_abs + 16 + r]
        low = 16 + r
        for w in range(1 + r, 16 + r):
            there = jnp.maximum(first_abs + w, 0)
            same = (docs_ref[there] == document) & (first_abs + w >= 0)
            low = low - same.astype(jnp.int32)
        start = (low - (1 + r)) // 2
        rows = pl.ds(r * BLK, BLK)
        for h in range(GROUP):
            cols = pl.ds(h * E, E)
            part = q_ref[rows, cols]
            qs_ref[pl.ds(h * BLK, BLK), :] = part
            qt_ref[:, pl.ds(h * BLK, BLK)] = part.T
        mx_ref[...] = jnp.full_like(mx_ref, -jnp.inf)

        def window(j):
            return pl.ds(pl.multiple_of((1 + r) * BLK + j * 2 * BLK, BLK), 2 * BLK)

        def score_step(j, extra, r=r, low=low):
            s = dot_nt(qs_ref[...], kv_ref[window(j), 0:E])
            block = (1 + r) + 2 * j + lane2 // BLK
            bias = jnp.where(block >= low, 0.0, -jnp.inf).astype(F32)
            for h in range(GROUP):
                part = s[h * BLK:(h + 1) * BLK] + bias
                left, right = part[:, :BLK], part[:, BLK:]
                if extra:
                    right = right + causal
                hr = pl.ds(h * BLK, BLK)
                s_ref[j, hr, 0:BLK] = left
                s_ref[j, hr, BLK:2 * BLK] = right
                mx_ref[hr, :] = jnp.maximum(mx_ref[hr, :], jnp.maximum(left, right))

        def score_body(j, c):
            score_step(j, False)
            return c
        lax.fori_loop(start, PAIRS - 1, score_body, 0)
        score_step(PAIRS - 1, True)

        for h in range(GROUP):
            hr = pl.ds(h * BLK, BLK)
            top = jnp.max(mx_ref[hr, :], axis=1, keepdims=True)
            st_ref[hr, :] = jnp.broadcast_to(top, (BLK, BLK))
        mx_ref[...] = jnp.zeros_like(mx_ref)
        acc_ref[...] = jnp.zeros_like(acc_ref)

        def out_body(j, c, r=r):
            kb = first_abs + (1 + r) + 2 * j
            kb = jnp.where(kb < 0, BLK - 1, kb)
            for h in range(GROUP):
                hr = pl.ds(h * BLK, BLK)
                top = st_ref[hr, :]
                left = jnp.exp2((s_ref[j, hr, 0:BLK] - top) * expo)
                right = jnp.exp2((s_ref[j, hr, BLK:2 * BLK] - top) * expo)
                s_ref[j, hr, 0:BLK] = left
                s_ref[j, hr, BLK:2 * BLK] = right
                mx_ref[hr, :] = mx_ref[hr, :] + (left + right)
                w_ref[j, hr, 0:BLK] = (left * keep_ref[h, pl.ds(kb, BLK), :]).astype(BF16)
                w_ref[j, hr, BLK:2 * BLK] = (right * keep_ref[h, pl.ds(kb + 1, BLK), :]).astype(BF16)
            acc_ref[...] += dot_nn(w_ref[j], kv_ref[window(j), E:2 * E])
            return c
        lax.fori_loop(start, PAIRS, out_body, 0)

        for h in range(GROUP):
            hr = pl.ds(h * BLK, BLK)
            cols = pl.ds(h * E, E)
            total = jnp.sum(mx_ref[hr, :], axis=1, keepdims=True)
            inverse = 1.0 / total
            o = (acc_ref[hr, :] * (inverse * scale)).astype(BF16)
            out_ref[rows, cols] = o
            grad = g_ref[rows, cols].astype(F32)
            delta = jnp.sum(grad * o.astype(F32), axis=1, keepdims=True) * inverse
            st_ref[hr, :] = jnp.broadcast_to(delta, (BLK, BLK))
            scaled = (grad * (inverse * scale)).astype(BF16)
            gs_ref[hr, :] = scaled
            gt_ref[:, hr] = scaled.T
        acc_ref[...] = jnp.zeros_like(acc_ref)

        def grad_body(j, c, r=r):
            kb = first_abs + (1 + r) + 2 * j
            kb = jnp.where(kb < 0, BLK - 1, kb)
            dw = dot_nt(gs_ref[...], kv_ref[window(j), E:2 * E])
            dvt_ref[:, window(j)] += dot_nn(gt_ref[...], w_ref[j])
            for h in range(GROUP):
                hr = pl.ds(h * BLK, BLK)
                delta = st_ref[hr, :]
                part = dw[h * BLK:(h + 1) * BLK]
                left = s_ref[j, hr, 0:BLK] * (part[:, :BLK] * keep_ref[h, pl.ds(kb, BLK), :] - delta)
                right = s_ref[j, hr, BLK:2 * BLK] * (part[:, BLK:] * keep_ref[h, pl.ds(kb + 1, BLK), :] - delta)
                w_ref[j, hr, 0:BLK] = left.astype(BF16)
                w_ref[j, hr, BLK:2 * BLK] = right.astype(BF16)
            acc_ref[...] += dot_nn(w_ref[j], kv_ref[window(j), 0:E])
            dkt_ref[:, window(j)] += dot_nn(qt_ref[...], w_ref[j])
            return c
        lax.fori_loop(start, PAIRS, grad_body, 0)

        for h in range(GROUP):
            hr = pl.ds(h * BLK, BLK)
            dq_ref[rows, pl.ds(h * E, E)] = (acc_ref[hr, :] * root).astype(BF16)

    for w in range(WIN // (2 * BLK)):
        cs = pl.ds(w * 2 * BLK, 2 * BLK)
        dkv_ref[cs, 0:E] = (dkt_ref[:, cs] * root).T.astype(BF16)
        dkv_ref[cs, E:2 * E] = dvt_ref[:, cs].T.astype(BF16)


def attention(docs, q, kv, g, bits):
    vm = pl.BlockSpec(memory_space=pltpu.VMEM)
    return pl.pallas_call(
        attn_kernel,
        out_shape=(jax.ShapeDtypeStruct((2 * BLK, GROUP * E), BF16),
                   jax.ShapeDtypeStruct((2 * BLK, GROUP * E), BF16),
                   jax.ShapeDtypeStruct((WIN, 2 * E), BF16)),
        in_specs=[pl.BlockSpec(memory_space=pltpu.SMEM), vm, vm, vm, vm],
        out_specs=(vm, vm, vm),
        scratch_shapes=[
            pltpu.VMEM((PAIRS, GROUP * BLK, 2 * BLK), F32),
            pltpu.VMEM((PAIRS, GROUP * BLK, 2 * BLK), BF16),
            pltpu.VMEM((GROUP, 2 * BLK, BLK), F32),
            pltpu.VMEM((GROUP * BLK, E), BF16),
            pltpu.VMEM((GROUP * BLK, E), BF16),
            pltpu.VMEM((E, GROUP * BLK), BF16),
            pltpu.VMEM((E, GROUP * BLK), BF16),
            pltpu.VMEM((GROUP * BLK, E), F32),
            pltpu.VMEM((GROUP * BLK, BLK), F32),
            pltpu.VMEM((E, WIN), F32),
            pltpu.VMEM((E, WIN), F32),
            pltpu.VMEM((GROUP * BLK, BLK), F32),
        ],
        cost_estimate=pl.CostEstimate(flops=6 * 10**9, bytes_accessed=6 * 10**6, transcendentals=4 * 10**6),
    )(docs, q, kv, g, bits)


def relay(blocks, relay_mask):
    count = lax.axis_size("ctx")

    def branch(mask):
        def move(block):
            if mask == 0:
                return block
            return lax.ppermute(block, "ctx", [(i, i ^ mask) for i in range(count)])
        return move

    moved = [lax.switch(relay_mask[r], [branch(m) for m in range(count)], blocks[r]) for r in range(2)]
    return jnp.concatenate(moved, axis=0)


def on_device(query, key, value, grad_out, doc_ids, relay_mask, drop_bits):
    q_local, window = gather_inputs(query, key, value)
    grads = relay(grad_out.reshape(2, BLK, GROUP * E), relay_mask)
    out, dq, dkv = attention(doc_ids, q_local, window.reshape(WIN, 2 * E), grads, drop_bits)
    out_bal = relay(out.reshape(2, BLK, GROUP * E), relay_mask)
    grad_q, grad_k, grad_v = scatter_grads(dkv.reshape(9, 2 * BLK, 2 * E), dq)
    return (out_bal, grad_q, grad_k, grad_v)


def solution(mesh):
    placed = (
        P(("ctx", "head"), None),
        P(("ctx", "head"), None),
        P(("ctx", "head"), None),
        P("ctx", "head"),
        P(),
        P(),
        P("head", None, None),
    )
    return jax.shard_map(
        on_device,
        mesh=mesh,
        in_specs=placed,
        out_specs=(
            P("ctx", "head"),
            P(("ctx", "head"), None),
            P(("ctx", "head"), None),
            P(("ctx", "head"), None),
        ),
        check_vma=False,
    )
```

```python
import math

import jax
import jax.numpy as jnp
from jax import lax
from jax.experimental import pallas as pl
from jax.experimental.pallas import tpu as pltpu
from jax.sharding import PartitionSpec as P

E = 128
BLK = 128
GROUP = 8
PAIRS = 8
WIN = 18 * BLK
NZ, NY, NH = 8, 4, 8
F32 = jnp.float32
BF16 = jnp.bfloat16
MESH = pl.DeviceIdType.MESH


def place():
    ctx, head = lax.axis_index("ctx"), lax.axis_index("head")
    return ctx // NY, ctx % NY, head


def remote(src, dst, send, recv, ctx, head):
    return pltpu.make_async_remote_copy(
        src_ref=src, dst_ref=dst, send_sem=send, recv_sem=recv,
        device_id=(ctx, head), device_id_type=MESH)


def greet(zi, yi, head):
    barrier = pltpu.get_barrier_semaphore()
    peers = [(zi * NY + yi, (head + d) % NH) for d in range(1, NH)]
    peers += [(((zi + d) % NZ) * NY + yi, head) for d in (1, 2, NZ - 1, NZ - 2)]
    peers += [(zi * NY + (yi + k) % NY, head) for k in range(1, NY)]
    for peer in peers:
        pl.semaphore_signal(barrier, inc=1, device_id=peer, device_id_type=MESH)
    pl.semaphore_wait(barrier, len(peers))


def ring_routes(count, rounds):
    tables = []
    for mask in range(count):
        flows = []
        for place in range(count):
            up = (place ^ mask) - place
            up %= count
            for piece in range(2):
                if up == 0:
                    continue
                down = count - up
                forward = up < down or (up == down and piece == 0)
                flows.append(dict(at=place, left=min(up, down), step=1 if forward else -1,
                                  slot=piece, piece=piece, goal=place ^ mask))
        sends = [[[0, 0] for _ in range(rounds)] for _ in range(count)]
        final = [[0, 1] for _ in range(count)]
        for t in range(rounds):
            moved = {}
            for flow in sorted(flows, key=lambda f: (-f["left"], f["piece"], f["at"])):
                if flow["left"] == 0:
                    continue
                way = 0 if flow["step"] == 1 else 1
                if (flow["at"], way) in moved:
                    continue
                moved[flow["at"], way] = flow
            for (at, way), flow in moved.items():
                sends[at][t][way] = flow["slot"]
                flow["at"] = (at + flow["step"]) % count
                flow["left"] -= 1
                flow["slot"] = 2 + 2 * t + way
                if flow["left"] == 0:
                    assert flow["at"] == flow["goal"]
                    final[flow["at"]][flow["piece"]] = flow["slot"]
        assert all(flow["left"] == 0 for flow in flows), (count, mask)
        for place in range(count):
            tables.append([s for pair in sends[place] for s in pair] + final[place])
    return tables

ZT, YT = 4, 2
Z_ROUTES = ring_routes(NZ, ZT)
Y_ROUTES = ring_routes(NY, YT)
Z_WIDE, Y_WIDE = 2 * ZT + 2, 2 * YT + 2
HALF = BLK // 2


def route_table():
    return jnp.array([v for row in Z_ROUTES + Y_ROUTES for v in row], jnp.int32)


def relay_scratch():
    half = (HALF, GROUP * E)
    dma = pltpu.SemaphoreType.DMA
    return ([pltpu.VMEM((2, ZT, 2) + half, BF16), pltpu.VMEM((2, YT, 2) + half, BF16)]
            + [pltpu.VMEM(half, BF16) for _ in range(2 * 2 * (ZT + YT))]
            + [pltpu.VMEM((2, 2) + half, BF16),
               dma((2, ZT, 2)), dma((2, ZT, 2)), dma((2, YT, 2)), dma((2, YT, 2))])


RELAY_COUNT = 2 + 2 * 2 * (ZT + YT) + 5


class Relay:
    def __init__(self, mask_ref, table_ref, src_ref, dst_ref, scratch, place_of):
        zi, yi, head = place_of
        self.src, self.dst = src_ref, dst_ref
        z_stage, y_stage = scratch[0], scratch[1]
        landing = scratch[2:-5]
        self.mid = scratch[-5]
        zs, zr, ys, yr = scratch[-4:]
        self.copies = []
        self.rings = []
        for r in range(2):
            mask = mask_ref[r]
            z_base = ((mask // NY) * NZ + zi) * Z_WIDE
            y_base = NZ * NZ * Z_WIDE + ((mask % NY) * NY + yi) * Y_WIDE
            low = r * 2 * (ZT + YT)
            z_ring = dict(
                rounds=ZT, stage=z_stage, land=landing[low:low + 2 * ZT], routes=Z_ROUTES,
                pick=[table_ref[z_base + i] for i in range(Z_WIDE)], send=zs, recv=zr,
                to=[(((zi + step) % NZ) * NY + yi, head) for step in (1, NZ - 1)])
            y_ring = dict(
                rounds=YT, stage=y_stage, land=landing[low + 2 * ZT:low + 2 * (ZT + YT)], routes=Y_ROUTES,
                pick=[table_ref[y_base + i] for i in range(Y_WIDE)], send=ys, recv=yr,
                to=[(zi * NY + (yi + step) % NY, head) for step in (1, NY - 1)])
            self.rings.append([z_ring, y_ring] if r == 0 else [y_ring, z_ring])
        self.plan = []
        for r in range(2):
            steps = []
            for which, ring in enumerate(self.rings[r]):
                steps += [(which, t) for t in range(ring["rounds"])]
            self.plan.append(steps)

    def value(self, r, which, slot):
        ring = self.rings[r][which]
        if slot >= 2:
            return ring["land"][slot - 2][...]
        if which == 0:
            return self.src[pl.ds(r * BLK + slot * HALF, HALF), :]
        return self.mid[r, slot]

    def choose(self, r, which, index):
        ring = self.rings[r][which]
        slots = sorted({row[index] for row in ring["routes"]})
        chosen = self.value(r, which, slots[0])
        for slot in slots[1:]:
            chosen = jnp.where(ring["pick"][index] == slot, self.value(r, which, slot), chosen)
        return chosen

    def settle(self, r, which):
        ring = self.rings[r][which]
        for copy in ring["last"]:
            copy.wait_recv()

    def close(self, r, which):
        self.settle(r, which)
        ring = self.rings[r][which]
        for piece in range(2):
            chosen = self.choose(r, which, 2 * ring["rounds"] + piece)
            if which == 0:
                self.mid[r, piece] = chosen
            else:
                self.dst[pl.ds(r * BLK + piece * HALF, HALF), :] = chosen

    def step(self, n):
        for r in range(2):
            which, t = self.plan[r][n]
            ring = self.rings[r][which]
            if t > 0:
                self.settle(r, which)
            elif which == 1:
                self.close(r, 0)
            ring["last"] = []
            for way in range(2):
                ring["stage"][r, t, way] = self.choose(r, which, 2 * t + way)
            for way in range(2):
                copy = remote(ring["stage"].at[r, t, way], ring["land"][2 * t + way],
                              ring["send"].at[r, t, way], ring["recv"].at[r, t, way], *ring["to"][way])
                copy.start()
                ring["last"].append(copy)
                self.copies.append(copy)

    def finish(self):
        for r in range(2):
            self.close(r, 1)

    def drain(self):
        for copy in self.copies:
            copy.wait_send()


def build_keep(bits_ref, keep_ref):
    row = lax.broadcasted_iota(jnp.int32, (32, BLK), 0)
    for h in range(GROUP):
        parts = []
        for w in range(4):
            words = jnp.broadcast_to(bits_ref[h, w:w + 1, :], (32, BLK))
            parts.append((lax.shift_right_logical(words, row) & 1).astype(F32))
        kept = jnp.concatenate(parts, axis=0).T
        keep_ref[h, 0:BLK] = kept
        keep_ref[h, BLK:2 * BLK] = kept


def gather_kernel(mask_ref, table_ref, q_ref, k_ref, v_ref, g_ref, bits_ref, qb_ref, win_ref, gb_ref, keep_ref,
                  kv_send, kv_recv, q_send, q_recv, z_send, z_recv, y_send, y_recv, own_sem, *scratch):
    zi, yi, head = place()
    ctx = zi * NY + yi
    move = Relay(mask_ref, table_ref, g_ref, gb_ref, scratch, (zi, yi, head))
    greet(zi, yi, head)
    mine = pl.ds(pl.multiple_of(head * 32, 32), 32)
    own = [
        pltpu.make_async_copy(k_ref.at[:, pl.ds(pl.multiple_of(head * E, E), E)],
                              win_ref.at[8, mine, pl.ds(0, E)], own_sem.at[0]),
        pltpu.make_async_copy(v_ref.at[:, pl.ds(pl.multiple_of(head * E, E), E)],
                              win_ref.at[8, mine, pl.ds(E, E)], own_sem.at[1]),
        pltpu.make_async_copy(q_ref.at[:, pl.ds(pl.multiple_of(head * GROUP * E, GROUP * E), GROUP * E)],
                              qb_ref.at[mine, :], own_sem.at[2]),
    ]
    for copy in own:
        copy.start()
    kv_copies = []
    for d in range(1, NH):
        to = (head + d) % NH
        cols = pl.ds(pl.multiple_of(to * E, E), E)
        for part, ref in enumerate((k_ref, v_ref)):
            copy = remote(ref.at[:, cols], win_ref.at[8, mine, pl.ds(part * E, E)],
                          kv_send.at[part, d], kv_recv.at[part, d], ctx, to)
            copy.start()
            kv_copies.append(copy)
    q_copies = []
    for d in range(1, NH):
        to = (head + d) % NH
        cols = pl.ds(pl.multiple_of(to * GROUP * E, GROUP * E), GROUP * E)
        copy = remote(q_ref.at[:, cols], qb_ref.at[mine, :], q_send.at[d], q_recv.at[d], ctx, to)
        copy.start()
        q_copies.append(copy)
    move.step(0)
    build_keep(bits_ref, keep_ref)
    own[0].wait()
    own[1].wait()
    for copy in kv_copies:
        copy.wait_recv()
    z_copies = []
    for d in (1, 2):
        copy = remote(win_ref.at[8], win_ref.at[8 - 4 * d], z_send.at[d], z_recv.at[d],
                      ((zi + d) % NZ) * NY + yi, head)
        copy.start()
        z_copies.append(copy)
    y_copies = []
    for part in range(2):
        for k in range(1, NY):
            wrap = (yi + k) // NY
            y_copies.append((part, k, wrap, remote(
                win_ref.at[8 - 4 * part - 4 * wrap], win_ref.at[8 - 4 * part - k],
                y_send.at[part, k], y_recv.at[part, k], zi * NY + (yi + k) % NY, head)))
    for part, k, wrap, copy in y_copies:
        if part == 0:
            @pl.when(wrap == 0)
            def _(copy=copy):
                copy.start()
    move.step(1)
    z_copies[0].wait_recv()
    for part, k, wrap, copy in y_copies:
        @pl.when(wrap == 1 - part)
        def _(copy=copy):
            copy.start()
    move.step(2)
    z_copies[1].wait_recv()
    for part, k, wrap, copy in y_copies:
        if part == 1:
            @pl.when(wrap == 1)
            def _(copy=copy):
                copy.start()
    for n in range(3, ZT + YT):
        move.step(n)
    move.finish()
    for copy in q_copies:
        copy.wait_recv()
    for _, _, _, copy in y_copies:
        copy.wait_recv()
    own[2].wait()
    move.drain()
    for copy in kv_copies + q_copies + z_copies:
        copy.wait_send()
    for _, _, _, copy in y_copies:
        copy.wait_send()


def gather_inputs(relay_mask, table, query, key, value, grads, bits):
    vm = pl.BlockSpec(memory_space=pltpu.VMEM)
    sm = pl.BlockSpec(memory_space=pltpu.SMEM)
    dma = pltpu.SemaphoreType.DMA
    return pl.pallas_call(
        gather_kernel,
        out_shape=(jax.ShapeDtypeStruct((2 * BLK, GROUP * E), BF16),
                   jax.ShapeDtypeStruct((9, 2 * BLK, 2 * E), BF16),
                   jax.ShapeDtypeStruct((2 * BLK, GROUP * E), BF16),
                   jax.ShapeDtypeStruct((GROUP, 2 * BLK, BLK), F32)),
        in_specs=[sm, sm, vm, vm, vm, vm, vm],
        out_specs=(vm, vm, vm, vm),
        scratch_shapes=[dma((2, NH)), dma((2, NH)), dma((NH,)), dma((NH,)), dma((3,)), dma((3,)),
                        dma((2, NY)), dma((2, NY)), dma((3,))] + relay_scratch(),
        compiler_params=pltpu.CompilerParams(collective_id=0, has_side_effects=True),
    )(relay_mask, table, query, key, value, grads, bits)


def scatter_kernel(mask_ref, table_ref, out_ref, dkv_ref, dq_ref, ob_ref, gq_ref, gk_ref, gv_ref,
                   r_ref, zs_ref, zr_ref, own_ref, fin_ref,
                   q_send, q_recv, y_send, y_recv, z_send, z_recv, kv_send, kv_recv, own_sem, *scratch):
    zi, yi, head = place()
    ctx = zi * NY + yi
    move = Relay(mask_ref, table_ref, out_ref, ob_ref, scratch, (zi, yi, head))
    greet(zi, yi, head)
    wide = pl.ds(pl.multiple_of(head * GROUP * E, GROUP * E), GROUP * E)
    slim = pl.ds(pl.multiple_of(head * E, E), E)
    y_copies = []
    for part in (1, 0):
        for k in range(1, NY):
            copy = remote(dkv_ref.at[8 - 4 * part - k], r_ref.at[part, k - 1],
                          y_send.at[part, k], y_recv.at[part, k],
                          zi * NY + (yi + NY - k) % NY, head)
            copy.start()
            y_copies.append(copy)
    move.step(0)
    q_copies = []
    for d in range(1, NH):
        to = (head + d) % NH
        rows = pl.ds(pl.multiple_of(to * 32, 32), 32)
        copy = remote(dq_ref.at[rows, :], gq_ref.at[:, wide], q_send.at[d], q_recv.at[d], ctx, to)
        copy.start()
        q_copies.append(copy)
    mine = pl.ds(pl.multiple_of(head * 32, 32), 32)
    own = [pltpu.make_async_copy(dq_ref.at[mine, :], gq_ref.at[:, wide], own_sem.at[0])]
    own[0].start()
    move.step(1)
    for copy in y_copies:
        copy.wait_recv()
    sums = [dkv_ref[8 - 4 * p].astype(F32) for p in range(3)]
    for k in range(1, NY):
        wraps = (yi + k) // NY > 0
        first, second = r_ref[0, k - 1].astype(F32), r_ref[1, k - 1].astype(F32)
        zero = jnp.zeros_like(first)
        sums[0] = sums[0] + jnp.where(wraps, zero, first)
        sums[1] = sums[1] + jnp.where(wraps, first, second)
        sums[2] = sums[2] + jnp.where(wraps, second, zero)
    zs_ref[0] = sums[1].astype(BF16)
    zs_ref[1] = sums[2].astype(BF16)
    own_ref[...] = sums[0]
    z_copies = []
    for d in (1, 2):
        copy = remote(zs_ref.at[d - 1], zr_ref.at[d - 1], z_send.at[d], z_recv.at[d],
                      ((zi + NZ - d) % NZ) * NY + yi, head)
        copy.start()
        z_copies.append(copy)
    move.step(2)
    move.step(3)
    for copy in z_copies:
        copy.wait_recv()
    fin_ref[...] = (own_ref[...] + zr_ref[0].astype(F32) + zr_ref[1].astype(F32)).astype(BF16)
    kv_copies = []
    for d in range(1, NH):
        to = (head + d) % NH
        rows = pl.ds(pl.multiple_of(to * 32, 32), 32)
        for part, ref in enumerate((gk_ref, gv_ref)):
            copy = remote(fin_ref.at[rows, pl.ds(part * E, E)], ref.at[:, slim],
                          kv_send.at[part, d], kv_recv.at[part, d], ctx, to)
            copy.start()
            kv_copies.append(copy)
    for part, ref in enumerate((gk_ref, gv_ref)):
        copy = pltpu.make_async_copy(fin_ref.at[mine, pl.ds(part * E, E)], ref.at[:, slim],
                                     own_sem.at[1 + part])
        copy.start()
        own.append(copy)
    move.step(4)
    move.step(5)
    move.finish()
    for copy in q_copies + kv_copies:
        copy.wait_recv()
    for copy in own:
        copy.wait()
    move.drain()
    for copy in q_copies + kv_copies + y_copies + z_copies:
        copy.wait_send()


def scatter_grads(relay_mask, table, out, dkv, dq):
    vm = pl.BlockSpec(memory_space=pltpu.VMEM)
    sm = pl.BlockSpec(memory_space=pltpu.SMEM)
    dma = pltpu.SemaphoreType.DMA
    return pl.pallas_call(
        scatter_kernel,
        out_shape=(jax.ShapeDtypeStruct((2 * BLK, GROUP * E), BF16),
                   jax.ShapeDtypeStruct((32, NH * GROUP * E), BF16),
                   jax.ShapeDtypeStruct((32, NH * E), BF16),
                   jax.ShapeDtypeStruct((32, NH * E), BF16)),
        in_specs=[sm, sm, vm, vm, vm],
        out_specs=(vm, vm, vm, vm),
        scratch_shapes=[
            pltpu.VMEM((2, NY - 1, 2 * BLK, 2 * E), BF16),
            pltpu.VMEM((2, 2 * BLK, 2 * E), BF16),
            pltpu.VMEM((2, 2 * BLK, 2 * E), BF16),
            pltpu.VMEM((2 * BLK, 2 * E), F32),
            pltpu.VMEM((2 * BLK, 2 * E), BF16),
            dma((NH,)), dma((NH,)), dma((2, NY)), dma((2, NY)), dma((3,)), dma((3,)),
            dma((2, NH)), dma((2, NH)), dma((3,))] + relay_scratch(),
        compiler_params=pltpu.CompilerParams(collective_id=1, has_side_effects=True),
    )(relay_mask, table, out, dkv, dq)


def dot_nt(a, b):
    return lax.dot_general(a, b, (((1,), (1,)), ((), ())), preferred_element_type=F32)


def dot_nn(a, b):
    return lax.dot_general(a, b, (((1,), (0,)), ((), ())), preferred_element_type=F32)


def attn_kernel(docs_ref, q_ref, kv_ref, g_ref, keep_ref, out_ref, dq_ref, dkv_ref,
                s_ref, w_ref, qs_ref, gs_ref, qt_ref, gt_ref, acc_ref, mx_ref,
                dkt_ref, dvt_ref, st_ref):
    root = 1.0 / math.sqrt(E)
    expo = root * math.log2(math.e)
    scale = 1.0 / 0.9
    lane = lax.broadcasted_iota(jnp.int32, (BLK, BLK), 1)
    row = lax.broadcasted_iota(jnp.int32, (BLK, BLK), 0)
    dkt_ref[...] = jnp.zeros_like(dkt_ref)
    dvt_ref[...] = jnp.zeros_like(dvt_ref)
    first_abs = 2 * lax.axis_index("ctx") - 16
    causal = jnp.where(lane <= row, 0.0, -jnp.inf).astype(F32)
    lane2 = lax.broadcasted_iota(jnp.int32, (1, 2 * BLK), 1)

    for r in range(2):
        document = docs_ref[first_abs + 16 + r]
        low = 16 + r
        for w in range(1 + r, 16 + r):
            there = jnp.maximum(first_abs + w, 0)
            same = (docs_ref[there] == document) & (first_abs + w >= 0)
            low = low - same.astype(jnp.int32)
        start = (low - (1 + r)) // 2
        rows = pl.ds(r * BLK, BLK)
        for h in range(GROUP):
            cols = pl.ds(h * E, E)
            part = q_ref[rows, cols]
            qs_ref[pl.ds(h * BLK, BLK), :] = part
            qt_ref[:, pl.ds(h * BLK, BLK)] = part.T
        mx_ref[...] = jnp.full_like(mx_ref, -jnp.inf)

        def window(j):
            return pl.ds(pl.multiple_of((1 + r) * BLK + j * 2 * BLK, BLK), 2 * BLK)

        def score_step(j, extra, r=r, low=low):
            s = dot_nt(qs_ref[...], kv_ref[window(j), 0:E])
            block = (1 + r) + 2 * j + lane2 // BLK
            bias = jnp.where(block >= low, 0.0, -jnp.inf).astype(F32)
            for h in range(GROUP):
                part = s[h * BLK:(h + 1) * BLK] + bias
                left, right = part[:, :BLK], part[:, BLK:]
                if extra:
                    right = right + causal
                hr = pl.ds(h * BLK, BLK)
                s_ref[j, hr, 0:BLK] = left
                s_ref[j, hr, BLK:2 * BLK] = right
                mx_ref[hr, :] = jnp.maximum(mx_ref[hr, :], jnp.maximum(left, right))

        def score_body(j, c):
            score_step(j, False)
            return c
        lax.fori_loop(start, PAIRS - 1, score_body, 0)
        score_step(PAIRS - 1, True)

        for h in range(GROUP):
            hr = pl.ds(h * BLK, BLK)
            top = jnp.max(mx_ref[hr, :], axis=1, keepdims=True)
            st_ref[hr, :] = jnp.broadcast_to(top, (BLK, BLK))
        mx_ref[...] = jnp.zeros_like(mx_ref)
        acc_ref[...] = jnp.zeros_like(acc_ref)

        def out_body(j, c, r=r):
            kb = first_abs + (1 + r) + 2 * j
            kb = jnp.where(kb < 0, BLK - 1, kb)
            for h in range(GROUP):
                hr = pl.ds(h * BLK, BLK)
                top = st_ref[hr, :]
                left = jnp.exp2((s_ref[j, hr, 0:BLK] - top) * expo)
                right = jnp.exp2((s_ref[j, hr, BLK:2 * BLK] - top) * expo)
                s_ref[j, hr, 0:BLK] = left
                s_ref[j, hr, BLK:2 * BLK] = right
                mx_ref[hr, :] = mx_ref[hr, :] + (left + right)
                w_ref[j, hr, 0:BLK] = (left * keep_ref[h, pl.ds(kb, BLK), :]).astype(BF16)
                w_ref[j, hr, BLK:2 * BLK] = (right * keep_ref[h, pl.ds(kb + 1, BLK), :]).astype(BF16)
            acc_ref[...] += dot_nn(w_ref[j], kv_ref[window(j), E:2 * E])
            return c
        lax.fori_loop(start, PAIRS, out_body, 0)

        for h in range(GROUP):
            hr = pl.ds(h * BLK, BLK)
            cols = pl.ds(h * E, E)
            total = jnp.sum(mx_ref[hr, :], axis=1, keepdims=True)
            inverse = 1.0 / total
            o = (acc_ref[hr, :] * (inverse * scale)).astype(BF16)
            out_ref[rows, cols] = o
            grad = g_ref[rows, cols].astype(F32)
            delta = jnp.sum(grad * o.astype(F32), axis=1, keepdims=True) * inverse
            st_ref[hr, :] = jnp.broadcast_to(delta, (BLK, BLK))
            scaled = (grad * (inverse * scale)).astype(BF16)
            gs_ref[hr, :] = scaled
            gt_ref[:, hr] = scaled.T
        acc_ref[...] = jnp.zeros_like(acc_ref)

        def grad_body(j, c, r=r):
            kb = first_abs + (1 + r) + 2 * j
            kb = jnp.where(kb < 0, BLK - 1, kb)
            dw = dot_nt(gs_ref[...], kv_ref[window(j), E:2 * E])
            dvt_ref[:, window(j)] += dot_nn(gt_ref[...], w_ref[j])
            for h in range(GROUP):
                hr = pl.ds(h * BLK, BLK)
                delta = st_ref[hr, :]
                part = dw[h * BLK:(h + 1) * BLK]
                left = s_ref[j, hr, 0:BLK] * (part[:, :BLK] * keep_ref[h, pl.ds(kb, BLK), :] - delta)
                right = s_ref[j, hr, BLK:2 * BLK] * (part[:, BLK:] * keep_ref[h, pl.ds(kb + 1, BLK), :] - delta)
                w_ref[j, hr, 0:BLK] = left.astype(BF16)
                w_ref[j, hr, BLK:2 * BLK] = right.astype(BF16)
            acc_ref[...] += dot_nn(w_ref[j], kv_ref[window(j), 0:E])
            dkt_ref[:, window(j)] += dot_nn(qt_ref[...], w_ref[j])
            return c
        lax.fori_loop(start, PAIRS, grad_body, 0)

        for h in range(GROUP):
            hr = pl.ds(h * BLK, BLK)
            dq_ref[rows, pl.ds(h * E, E)] = (acc_ref[hr, :] * root).astype(BF16)

    for w in range(WIN // (2 * BLK)):
        cs = pl.ds(w * 2 * BLK, 2 * BLK)
        dkv_ref[cs, 0:E] = (dkt_ref[:, cs] * root).T.astype(BF16)
        dkv_ref[cs, E:2 * E] = dvt_ref[:, cs].T.astype(BF16)


def attention(docs, q, kv, g, keep):
    vm = pl.BlockSpec(memory_space=pltpu.VMEM)
    return pl.pallas_call(
        attn_kernel,
        out_shape=(jax.ShapeDtypeStruct((2 * BLK, GROUP * E), BF16),
                   jax.ShapeDtypeStruct((2 * BLK, GROUP * E), BF16),
                   jax.ShapeDtypeStruct((WIN, 2 * E), BF16)),
        in_specs=[pl.BlockSpec(memory_space=pltpu.SMEM), vm, vm, vm, vm],
        out_specs=(vm, vm, vm),
        scratch_shapes=[
            pltpu.VMEM((PAIRS, GROUP * BLK, 2 * BLK), F32),
            pltpu.VMEM((PAIRS, GROUP * BLK, 2 * BLK), BF16),
            pltpu.VMEM((GROUP * BLK, E), BF16),
            pltpu.VMEM((GROUP * BLK, E), BF16),
            pltpu.VMEM((E, GROUP * BLK), BF16),
            pltpu.VMEM((E, GROUP * BLK), BF16),
            pltpu.VMEM((GROUP * BLK, E), F32),
            pltpu.VMEM((GROUP * BLK, BLK), F32),
            pltpu.VMEM((E, WIN), F32),
            pltpu.VMEM((E, WIN), F32),
            pltpu.VMEM((GROUP * BLK, BLK), F32),
        ],
        cost_estimate=pl.CostEstimate(flops=6 * 10**9, bytes_accessed=6 * 10**6, transcendentals=4 * 10**6),
    )(docs, q, kv, g, keep)


def on_device(query, key, value, grad_out, doc_ids, relay_mask, drop_bits):
    table = route_table()
    q_local, window, grads, keep = gather_inputs(
        relay_mask, table, query, key, value, grad_out, drop_bits.transpose(0, 2, 1))
    out, dq, dkv = attention(doc_ids, q_local, window.reshape(WIN, 2 * E), grads, keep)
    return scatter_grads(relay_mask, table, out, dkv.reshape(9, 2 * BLK, 2 * E), dq)


def solution(mesh):
    placed = (
        P(("ctx", "head"), None),
        P(("ctx", "head"), None),
        P(("ctx", "head"), None),
        P("ctx", "head"),
        P(),
        P(),
        P("head", None, None),
    )
    return jax.shard_map(
        on_device,
        mesh=mesh,
        in_specs=placed,
        out_specs=(
            P("ctx", "head"),
            P(("ctx", "head"), None),
            P(("ctx", "head"), None),
            P(("ctx", "head"), None),
        ),
        check_vma=False,
    )
```

```python
import math

import jax
import jax.numpy as jnp
from jax import lax
from jax.experimental import pallas as pl
from jax.experimental.pallas import tpu as pltpu
from jax.sharding import PartitionSpec as P

E = 128
BLK = 128
GROUP = 8
PAIRS = 8
WIN = 18 * BLK
NZ, NY, NH = 8, 4, 8
F32 = jnp.float32
BF16 = jnp.bfloat16
MESH = pl.DeviceIdType.MESH


def place():
    ctx, head = lax.axis_index("ctx"), lax.axis_index("head")
    return ctx // NY, ctx % NY, head


def remote(src, dst, send, recv, ctx, head):
    return pltpu.make_async_remote_copy(
        src_ref=src, dst_ref=dst, send_sem=send, recv_sem=recv,
        device_id=(ctx, head), device_id_type=MESH)


def greet(zi, yi, head):
    barrier = pltpu.get_barrier_semaphore()
    peers = [(zi * NY + yi, (head + d) % NH) for d in range(1, NH)]
    peers += [(((zi + d) % NZ) * NY + yi, head) for d in (1, 2, NZ - 1, NZ - 2)]
    peers += [(zi * NY + (yi + k) % NY, head) for k in range(1, NY)]
    for peer in peers:
        pl.semaphore_signal(barrier, inc=1, device_id=peer, device_id_type=MESH)
    pl.semaphore_wait(barrier, len(peers))


def ring_routes(count, rounds):
    tables = []
    for mask in range(count):
        flows = []
        for place in range(count):
            up = (place ^ mask) - place
            up %= count
            for piece in range(2):
                if up == 0:
                    continue
                down = count - up
                forward = up < down or (up == down and piece == 0)
                flows.append(dict(at=place, left=min(up, down), step=1 if forward else -1,
                                  slot=piece, piece=piece, goal=place ^ mask))
        sends = [[[0, 0] for _ in range(rounds)] for _ in range(count)]
        final = [[0, 1] for _ in range(count)]
        for t in range(rounds):
            moved = {}
            for flow in sorted(flows, key=lambda f: (-f["left"], f["piece"], f["at"])):
                if flow["left"] == 0:
                    continue
                way = 0 if flow["step"] == 1 else 1
                if (flow["at"], way) in moved:
                    continue
                moved[flow["at"], way] = flow
            for (at, way), flow in moved.items():
                sends[at][t][way] = flow["slot"]
                flow["at"] = (at + flow["step"]) % count
                flow["left"] -= 1
                flow["slot"] = 2 + 2 * t + way
                if flow["left"] == 0:
                    assert flow["at"] == flow["goal"]
                    final[flow["at"]][flow["piece"]] = flow["slot"]
        assert all(flow["left"] == 0 for flow in flows), (count, mask)
        for place in range(count):
            tables.append([s for pair in sends[place] for s in pair] + final[place])
    return tables

ZT, YT = 4, 2
Z_ROUTES = ring_routes(NZ, ZT)
Y_ROUTES = ring_routes(NY, YT)
Z_WIDE, Y_WIDE = 2 * ZT + 2, 2 * YT + 2
STEPS = ZT + YT
HALF = BLK // 2
SPAN = GROUP * E // 2
STREAMS = ((0, 0, "zy"), (1, 0, "yz"), (0, 1, "yz"), (1, 1, "zy"))


def route_table():
    return jnp.array([v for row in Z_ROUTES + Y_ROUTES for v in row], jnp.int32)


def relay_scratch():
    count = len(STREAMS)
    dma = pltpu.SemaphoreType.DMA
    piece = (HALF, SPAN)
    return [pltpu.VMEM((count, ZT, 2) + piece, BF16), pltpu.VMEM((count, ZT, 2) + piece, BF16),
            pltpu.VMEM((count, YT, 2) + piece, BF16), pltpu.VMEM((count, YT, 2) + piece, BF16),
            pltpu.VMEM((count, 2) + piece, BF16),
            dma((count, ZT, 2)), dma((count, ZT, 2)), dma((count, YT, 2)), dma((count, YT, 2))]


RELAY_REFS = 9


class Relay:
    def __init__(self, mask_ref, table_ref, src_ref, dst_ref, scratch, place_of):
        zi, yi, head = place_of
        z_stage, z_land, y_stage, y_land, self.mid, zs, zr, ys, yr = scratch
        self.src, self.dst = src_ref, dst_ref
        self.copies = []
        self.rings = []
        self.plan = []
        for n, (r, _, order) in enumerate(STREAMS):
            mask = mask_ref[r]
            z_base = ((mask // NY) * NZ + zi) * Z_WIDE
            y_base = NZ * NZ * Z_WIDE + ((mask % NY) * NY + yi) * Y_WIDE
            rings = dict(
                z=dict(rounds=ZT, stage=z_stage, land=z_land, routes=Z_ROUTES, send=zs, recv=zr,
                       pick=[table_ref[z_base + i] for i in range(Z_WIDE)],
                       to=[(((zi + step) % NZ) * NY + yi, head) for step in (1, NZ - 1)]),
                y=dict(rounds=YT, stage=y_stage, land=y_land, routes=Y_ROUTES, send=ys, recv=yr,
                       pick=[table_ref[y_base + i] for i in range(Y_WIDE)],
                       to=[(zi * NY + (yi + step) % NY, head) for step in (1, NY - 1)]))
            self.rings.append([rings[axis] for axis in order])
            self.plan.append([(which, t) for which in range(2)
                              for t in range(self.rings[n][which]["rounds"])])

    def region(self, n, piece):
        r, part, _ = STREAMS[n]
        return pl.ds(r * BLK + piece * HALF, HALF), pl.ds(part * SPAN, SPAN)

    def value(self, n, which, slot):
        ring = self.rings[n][which]
        if slot >= 2:
            return ring["land"][n, (slot - 2) // 2, slot % 2]
        if which == 0:
            return self.src[self.region(n, slot)]
        return self.mid[n, slot]

    def choose(self, n, which, index):
        ring = self.rings[n][which]
        slots = sorted({row[index] for row in ring["routes"]})
        chosen = self.value(n, which, slots[0])
        for slot in slots[1:]:
            chosen = jnp.where(ring["pick"][index] == slot, self.value(n, which, slot), chosen)
        return chosen

    def close(self, n, which):
        ring = self.rings[n][which]
        for copy in ring["last"]:
            copy.wait_recv()
        for piece in range(2):
            chosen = self.choose(n, which, 2 * ring["rounds"] + piece)
            if which == 0:
                self.mid[n, piece] = chosen
            else:
                self.dst[self.region(n, piece)] = chosen

    def step(self, k):
        for n in range(len(STREAMS)):
            which, t = self.plan[n][k]
            ring = self.rings[n][which]
            if t > 0:
                for copy in ring["last"]:
                    copy.wait_recv()
            elif which == 1:
                self.close(n, 0)
            ring["last"] = []
            for way in range(2):
                ring["stage"][n, t, way] = self.choose(n, which, 2 * t + way)
            for way in range(2):
                copy = remote(ring["stage"].at[n, t, way], ring["land"].at[n, t, way],
                              ring["send"].at[n, t, way], ring["recv"].at[n, t, way], *ring["to"][way])
                copy.start()
                ring["last"].append(copy)
                self.copies.append(copy)

    def finish(self):
        for n in range(len(STREAMS)):
            self.close(n, 1)

    def drain(self):
        for copy in self.copies:
            copy.wait_send()


def build_keep(bits_ref, keep_ref):
    row = lax.broadcasted_iota(jnp.int32, (32, BLK), 0)
    for h in range(GROUP):
        parts = []
        for w in range(4):
            words = jnp.broadcast_to(bits_ref[h, w:w + 1, :], (32, BLK))
            parts.append((lax.shift_right_logical(words, row) & 1).astype(F32))
        kept = jnp.concatenate(parts, axis=0).T
        keep_ref[h, 0:BLK] = kept
        keep_ref[h, BLK:2 * BLK] = kept


def dot_nt(a, b):
    return lax.dot_general(a, b, (((1,), (1,)), ((), ())), preferred_element_type=F32)


def dot_nn(a, b):
    return lax.dot_general(a, b, (((1,), (0,)), ((), ())), preferred_element_type=F32)


class Attention:
    def __init__(self, docs_ref, q_ref, kv_ref, g_ref, keep_ref, out_ref, dq_ref, dkv_ref, scratch):
        (self.s, self.w, self.qs, self.qt, self.gs, self.gt, self.acc, self.mx, self.st, self.inv,
         self.dkt, self.dvt) = scratch
        self.docs, self.q, self.kv, self.g, self.keep = docs_ref, q_ref, kv_ref, g_ref, keep_ref
        self.out, self.dq, self.dkv = out_ref, dq_ref, dkv_ref
        self.first = 2 * lax.axis_index("ctx") - 16

    def part(self, r, j, left):
        cols = slice(0, E) if left else slice(E, 2 * E)
        if r == 1:
            return self.kv[j + 1, :, cols]
        return jnp.concatenate([self.kv[j, BLK:2 * BLK, cols], self.kv[j + 1, 0:BLK, cols]], axis=0)

    def columns(self, r, j):
        return pl.ds(pl.multiple_of((1 + r) * BLK + j * 2 * BLK, BLK), 2 * BLK)

    def forward(self, r):
        expo = math.log2(math.e) / math.sqrt(E)
        scale = 1.0 / 0.9
        lane = lax.broadcasted_iota(jnp.int32, (BLK, BLK), 1)
        row = lax.broadcasted_iota(jnp.int32, (BLK, BLK), 0)
        causal = jnp.where(lane <= row, 0.0, -jnp.inf).astype(F32)
        lane2 = lax.broadcasted_iota(jnp.int32, (1, 2 * BLK), 1)
        document = self.docs[self.first + 16 + r]
        low = 16 + r
        for w in range(1 + r, 16 + r):
            there = jnp.maximum(self.first + w, 0)
            same = jnp.where(self.docs[there] == document, 1, 0)
            low = low - jnp.where(self.first + w >= 0, same, 0)
        rows = pl.ds(r * BLK, BLK)
        for h in range(GROUP):
            part = self.q[rows, pl.ds(h * E, E)]
            self.qs[r, pl.ds(h * BLK, BLK), :] = part
            self.qt[r, :, pl.ds(h * BLK, BLK)] = part.T
        self.mx[...] = jnp.full_like(self.mx, -jnp.inf)

        def score_step(j, extra):
            s = dot_nt(self.qs[r], self.part(r, j, True))
            block = (1 + r) + 2 * j + lane2 // BLK
            bias = jnp.where(block >= low, 0.0, -jnp.inf).astype(F32)
            for h in range(GROUP):
                part = s[h * BLK:(h + 1) * BLK] + bias
                left, right = part[:, :BLK], part[:, BLK:]
                if extra:
                    right = right + causal
                hr = pl.ds(h * BLK, BLK)
                self.s[r, j, hr, 0:BLK] = left
                self.s[r, j, hr, BLK:2 * BLK] = right
                self.mx[hr, :] = jnp.maximum(self.mx[hr, :], jnp.maximum(left, right))

        def score_body(j, c):
            score_step(j, False)
            return c
        lax.fori_loop(0, PAIRS - 1, score_body, 0)
        score_step(PAIRS - 1, True)

        for h in range(GROUP):
            hr = pl.ds(h * BLK, BLK)
            top = jnp.max(self.mx[hr, :], axis=1, keepdims=True)
            self.st[hr, :] = jnp.broadcast_to(top, (BLK, BLK))
        self.mx[...] = jnp.zeros_like(self.mx)
        self.acc[...] = jnp.zeros_like(self.acc)

        def out_body(j, c):
            kb = self.table_row(r, j)
            for h in range(GROUP):
                hr = pl.ds(h * BLK, BLK)
                top = self.st[hr, :]
                left = jnp.exp2((self.s[r, j, hr, 0:BLK] - top) * expo)
                right = jnp.exp2((self.s[r, j, hr, BLK:2 * BLK] - top) * expo)
                self.s[r, j, hr, 0:BLK] = left
                self.s[r, j, hr, BLK:2 * BLK] = right
                self.mx[hr, :] = self.mx[hr, :] + (left + right)
                self.w[r, j, hr, 0:BLK] = (left * self.keep[h, pl.ds(kb, BLK), :]).astype(BF16)
                self.w[r, j, hr, BLK:2 * BLK] = (right * self.keep[h, pl.ds(kb + 1, BLK), :]).astype(BF16)
            self.acc[...] += dot_nn(self.w[r, j], self.part(r, j, False))
            return c
        lax.fori_loop(0, PAIRS, out_body, 0)

        for h in range(GROUP):
            hr = pl.ds(h * BLK, BLK)
            total = jnp.sum(self.mx[hr, :], axis=1, keepdims=True)
            inverse = 1.0 / total
            self.out[rows, pl.ds(h * E, E)] = (self.acc[hr, :] * (inverse * scale)).astype(BF16)
            self.inv[r, hr, :] = jnp.broadcast_to(inverse, (BLK, BLK))

    def table_row(self, r, j):
        kb = self.first + (1 + r) + 2 * j
        return jnp.where(kb < 0, BLK - 1, kb)

    def prepare(self, r):
        scale = 1.0 / 0.9
        rows = pl.ds(r * BLK, BLK)
        for h in range(GROUP):
            hr = pl.ds(h * BLK, BLK)
            cols = pl.ds(h * E, E)
            inverse = self.inv[r, hr, :]
            grad = self.g[rows, cols].astype(F32)
            delta = jnp.sum(grad * self.out[rows, cols].astype(F32), axis=1, keepdims=True)
            self.st[hr, :] = delta * inverse
            scaled = (grad * (inverse * scale)).astype(BF16)
            self.gs[hr, :] = scaled
            self.gt[:, hr] = scaled.T
        self.acc[...] = jnp.zeros_like(self.acc)

    def backward(self, r, begin, end):
        def grad_body(j, c):
            kb = self.table_row(r, j)
            dw = dot_nt(self.gs[...], self.part(r, j, False))
            self.dvt[:, self.columns(r, j)] += dot_nn(self.gt[...], self.w[r, j])
            for h in range(GROUP):
                hr = pl.ds(h * BLK, BLK)
                delta = self.st[hr, :]
                part = dw[h * BLK:(h + 1) * BLK]
                left = self.s[r, j, hr, 0:BLK] * (part[:, :BLK] * self.keep[h, pl.ds(kb, BLK), :] - delta)
                right = self.s[r, j, hr, BLK:2 * BLK] * (
                    part[:, BLK:] * self.keep[h, pl.ds(kb + 1, BLK), :] - delta)
                self.w[r, j, hr, 0:BLK] = left.astype(BF16)
                self.w[r, j, hr, BLK:2 * BLK] = right.astype(BF16)
            self.acc[...] += dot_nn(self.w[r, j], self.part(r, j, True))
            self.dkt[:, self.columns(r, j)] += dot_nn(self.qt[r], self.w[r, j])
            return c
        lax.fori_loop(begin, end, grad_body, 0)

    def store_query_grad(self, r):
        for h in range(GROUP):
            hr = pl.ds(h * BLK, BLK)
            self.dq[pl.ds(r * BLK, BLK), pl.ds(h * E, E)] = (self.acc[hr, :] * (1.0 / math.sqrt(E))).astype(BF16)

    def store_slot(self, slot):
        cs = pl.ds(slot * 2 * BLK, 2 * BLK)
        self.dkv[slot, :, 0:E] = (self.dkt[:, cs] * (1.0 / math.sqrt(E))).T.astype(BF16)
        self.dkv[slot, :, E:2 * E] = self.dvt[:, cs].T.astype(BF16)


def attn_scratch():
    rows = GROUP * BLK
    return [pltpu.VMEM((2, PAIRS, rows, 2 * BLK), F32),
            pltpu.VMEM((2, PAIRS, rows, 2 * BLK), BF16),
            pltpu.VMEM((2, rows, E), BF16),
            pltpu.VMEM((2, E, rows), BF16),
            pltpu.VMEM((rows, E), BF16),
            pltpu.VMEM((E, rows), BF16),
            pltpu.VMEM((rows, E), F32),
            pltpu.VMEM((rows, BLK), F32),
            pltpu.VMEM((rows, BLK), F32),
            pltpu.VMEM((2, rows, BLK), F32),
            pltpu.VMEM((E, WIN), F32),
            pltpu.VMEM((E, WIN), F32)]


def whole_kernel(docs_ref, mask_ref, table_ref, q_ref, k_ref, v_ref, g_ref, bits_ref,
                 ob_ref, gq_ref, gk_ref, gv_ref,
                 qb_ref, win_ref, gb_ref, keep_ref, out_ref, dq_ref, dkv_ref,
                 r_ref, zs_ref, zr_ref, own_ref, fin_ref,
                 kv_send, kv_recv, q_send, q_recv, z_send, z_recv, y_send, y_recv, own_sem,
                 dkv_send, dkv_recv, dq_send, dq_recv, dz_send, dz_recv, dy_send, dy_recv, down_sem,
                 *scratch):
    zi, yi, head = place()
    ctx = zi * NY + yi
    spot = (zi, yi, head)
    grad_move = Relay(mask_ref, table_ref, g_ref, gb_ref, scratch[:RELAY_REFS], spot)
    out_move = Relay(mask_ref, table_ref, out_ref, ob_ref, scratch[RELAY_REFS:2 * RELAY_REFS], spot)
    attn = Attention(docs_ref, qb_ref, win_ref, gb_ref, keep_ref, out_ref, dq_ref, dkv_ref,
                     scratch[2 * RELAY_REFS:])
    mine = pl.ds(pl.multiple_of(head * 32, 32), 32)
    wide = pl.ds(pl.multiple_of(head * GROUP * E, GROUP * E), GROUP * E)
    slim = pl.ds(pl.multiple_of(head * E, E), E)
    greet(zi, yi, head)

    own = [
        pltpu.make_async_copy(k_ref.at[:, slim], win_ref.at[8, mine, pl.ds(0, E)], own_sem.at[0]),
        pltpu.make_async_copy(v_ref.at[:, slim], win_ref.at[8, mine, pl.ds(E, E)], own_sem.at[1]),
        pltpu.make_async_copy(q_ref.at[:, wide], qb_ref.at[mine, :], own_sem.at[2]),
    ]
    for copy in own:
        copy.start()
    kv_copies = []
    for d in range(1, NH):
        to = (head + d) % NH
        cols = pl.ds(pl.multiple_of(to * E, E), E)
        for part, ref in enumerate((k_ref, v_ref)):
            copy = remote(ref.at[:, cols], win_ref.at[8, mine, pl.ds(part * E, E)],
                          kv_send.at[part, d], kv_recv.at[part, d], ctx, to)
            copy.start()
            kv_copies.append(copy)
    q_copies = []
    for d in range(1, NH):
        to = (head + d) % NH
        cols = pl.ds(pl.multiple_of(to * GROUP * E, GROUP * E), GROUP * E)
        copy = remote(q_ref.at[:, cols], qb_ref.at[mine, :], q_send.at[d], q_recv.at[d], ctx, to)
        copy.start()
        q_copies.append(copy)
    grad_move.step(0)
    build_keep(bits_ref, keep_ref)
    attn.dkt[...] = jnp.zeros_like(attn.dkt)
    attn.dvt[...] = jnp.zeros_like(attn.dvt)
    own[0].wait()
    own[1].wait()
    for copy in kv_copies:
        copy.wait_recv()
    z_copies = []
    for d in (1, 2):
        copy = remote(win_ref.at[8], win_ref.at[8 - 4 * d], z_send.at[d], z_recv.at[d],
                      ((zi + d) % NZ) * NY + yi, head)
        copy.start()
        z_copies.append(copy)
    y_copies = []
    for part in range(2):
        for k in range(1, NY):
            wrap = (yi + k) // NY
            y_copies.append((part, k, wrap, remote(
                win_ref.at[8 - 4 * part - 4 * wrap], win_ref.at[8 - 4 * part - k],
                y_send.at[part, k], y_recv.at[part, k], zi * NY + (yi + k) % NY, head)))
    for part, k, wrap, copy in y_copies:
        if part == 0:
            @pl.when(wrap == 0)
            def _(copy=copy):
                copy.start()
    z_copies[0].wait_recv()
    for part, k, wrap, copy in y_copies:
        @pl.when(wrap == 1 - part)
        def _(copy=copy):
            copy.start()
    grad_move.step(1)
    z_copies[1].wait_recv()
    for part, k, wrap, copy in y_copies:
        if part == 1:
            @pl.when(wrap == 1)
            def _(copy=copy):
                copy.start()
    grad_move.step(2)
    for copy in q_copies:
        copy.wait_recv()
    own[2].wait()
    for _, _, _, copy in y_copies:
        copy.wait_recv()

    grad_move.step(3)
    attn.forward(0)
    grad_move.step(4)
    attn.forward(1)
    grad_move.step(5)
    out_move.step(0)
    grad_move.finish()

    dq_copies = []

    def send_query_grads(r):
        for d in range(1, NH):
            to = (head + d) % NH
            rows = pl.ds(pl.multiple_of(to * 32, 32), 32)
            copy = remote(dq_ref.at[rows, :], gq_ref.at[:, wide], dq_send.at[d], dq_recv.at[d], ctx, to)
            if r == 0:
                dq_copies.append(copy)

            @pl.when(to // (NH // 2) == r)
            def _(copy=copy):
                copy.start()

    dy_copies = []

    def send_slots(part):
        for k in range(1, NY):
            slot = 8 - 4 * part - k
            attn.store_slot(slot)
            copy = remote(dkv_ref.at[slot], r_ref.at[part, k - 1],
                          dy_send.at[part, k], dy_recv.at[part, k], zi * NY + (yi + NY - k) % NY, head)
            copy.start()
            dy_copies.append(copy)

    attn.prepare(0)
    attn.backward(0, 0, PAIRS // 2)
    out_move.step(1)
    attn.backward(0, PAIRS // 2, PAIRS)
    attn.store_query_grad(0)
    send_query_grads(0)
    out_move.step(2)
    attn.prepare(1)
    attn.backward(1, 0, PAIRS // 2)
    send_slots(1)
    out_move.step(3)
    attn.backward(1, PAIRS // 2, PAIRS)
    send_slots(0)
    attn.store_query_grad(1)
    send_query_grads(1)
    for slot in (0, 4, 8):
        attn.store_slot(slot)
    down = [pltpu.make_async_copy(dq_ref.at[mine, :], gq_ref.at[:, wide], down_sem.at[0])]
    down[0].start()
    out_move.step(4)

    for copy in dy_copies:
        copy.wait_recv()
    sums = [dkv_ref[8 - 4 * p].astype(F32) for p in range(3)]
    for k in range(1, NY):
        wraps = (yi + k) // NY > 0
        first, second = r_ref[0, k - 1].astype(F32), r_ref[1, k - 1].astype(F32)
        zero = jnp.zeros_like(first)
        sums[0] = sums[0] + jnp.where(wraps, zero, first)
        sums[1] = sums[1] + jnp.where(wraps, first, second)
        sums[2] = sums[2] + jnp.where(wraps, second, zero)
    zs_ref[0] = sums[1].astype(BF16)
    zs_ref[1] = sums[2].astype(BF16)
    own_ref[...] = sums[0]
    dz_copies = []
    for d in (2, 1):
        copy = remote(zs_ref.at[d - 1], zr_ref.at[d - 1], dz_send.at[d], dz_recv.at[d],
                      ((zi + NZ - d) % NZ) * NY + yi, head)
        copy.start()
        dz_copies.append(copy)
    out_move.step(5)
    for copy in dz_copies:
        copy.wait_recv()
    fin_ref[...] = (own_ref[...] + zr_ref[0].astype(F32) + zr_ref[1].astype(F32)).astype(BF16)
    dkv_copies = []
    for d in range(1, NH):
        to = (head + d) % NH
        rows = pl.ds(pl.multiple_of(to * 32, 32), 32)
        for part, ref in enumerate((gk_ref, gv_ref)):
            copy = remote(fin_ref.at[rows, pl.ds(part * E, E)], ref.at[:, slim],
                          dkv_send.at[part, d], dkv_recv.at[part, d], ctx, to)
            copy.start()
            dkv_copies.append(copy)
    for part, ref in enumerate((gk_ref, gv_ref)):
        copy = pltpu.make_async_copy(fin_ref.at[mine, pl.ds(part * E, E)], ref.at[:, slim],
                                     down_sem.at[1 + part])
        copy.start()
        down.append(copy)
    out_move.finish()
    for copy in dq_copies + dkv_copies:
        copy.wait_recv()
    for copy in down:
        copy.wait()
    grad_move.drain()
    out_move.drain()
    for copy in kv_copies + q_copies + z_copies + dq_copies + dkv_copies + dy_copies + dz_copies:
        copy.wait_send()
    for _, _, _, copy in y_copies:
        copy.wait_send()


def on_device(query, key, value, grad_out, doc_ids, relay_mask, drop_bits):
    vm = pl.BlockSpec(memory_space=pltpu.VMEM)
    sm = pl.BlockSpec(memory_space=pltpu.SMEM)
    dma = pltpu.SemaphoreType.DMA
    links = [dma((2, NH)), dma((2, NH)), dma((NH,)), dma((NH,)), dma((3,)), dma((3,)),
             dma((2, NY)), dma((2, NY)), dma((3,))]
    return pl.pallas_call(
        whole_kernel,
        out_shape=(jax.ShapeDtypeStruct((2 * BLK, GROUP * E), BF16),
                   jax.ShapeDtypeStruct((32, NH * GROUP * E), BF16),
                   jax.ShapeDtypeStruct((32, NH * E), BF16),
                   jax.ShapeDtypeStruct((32, NH * E), BF16)),
        in_specs=[sm, sm, sm, vm, vm, vm, vm, vm],
        out_specs=(vm, vm, vm, vm),
        scratch_shapes=[
            pltpu.VMEM((2 * BLK, GROUP * E), BF16),
            pltpu.VMEM((9, 2 * BLK, 2 * E), BF16),
            pltpu.VMEM((2 * BLK, GROUP * E), BF16),
            pltpu.VMEM((GROUP, 2 * BLK, BLK), F32),
            pltpu.VMEM((2 * BLK, GROUP * E), BF16),
            pltpu.VMEM((2 * BLK, GROUP * E), BF16),
            pltpu.VMEM((9, 2 * BLK, 2 * E), BF16),
            pltpu.VMEM((2, NY - 1, 2 * BLK, 2 * E), BF16),
            pltpu.VMEM((2, 2 * BLK, 2 * E), BF16),
            pltpu.VMEM((2, 2 * BLK, 2 * E), BF16),
            pltpu.VMEM((2 * BLK, 2 * E), F32),
            pltpu.VMEM((2 * BLK, 2 * E), BF16),
        ] + links + links + relay_scratch() + relay_scratch() + attn_scratch(),
        compiler_params=pltpu.CompilerParams(
            collective_id=0, has_side_effects=True, vmem_limit_bytes=60 * 1024 * 1024),
    )(doc_ids, relay_mask, route_table(), query, key, value, grad_out, drop_bits.transpose(0, 2, 1))


def solution(mesh):
    placed = (
        P(("ctx", "head"), None),
        P(("ctx", "head"), None),
        P(("ctx", "head"), None),
        P("ctx", "head"),
        P(),
        P(),
        P("head", None, None),
    )
    return jax.shard_map(
        on_device,
        mesh=mesh,
        in_specs=placed,
        out_specs=(
            P("ctx", "head"),
            P(("ctx", "head"), None),
            P(("ctx", "head"), None),
            P(("ctx", "head"), None),
        ),
        check_vma=False,
    )
```

```python
import math

import jax
import jax.numpy as jnp
from jax import lax
from jax.experimental import pallas as pl
from jax.experimental.pallas import tpu as pltpu
from jax.sharding import PartitionSpec as P

E = 128
BLK = 128
GROUP = 8
PAIRS = 8
WIN = 18 * BLK
NZ, NY, NH = 8, 4, 8
F32 = jnp.float32
BF16 = jnp.bfloat16
MESH = pl.DeviceIdType.MESH


def place():
    ctx, head = lax.axis_index("ctx"), lax.axis_index("head")
    return ctx // NY, ctx % NY, head


def remote(src, dst, send, recv, ctx, head):
    return pltpu.make_async_remote_copy(
        src_ref=src, dst_ref=dst, send_sem=send, recv_sem=recv,
        device_id=(ctx, head), device_id_type=MESH)


def greet(zi, yi, head):
    barrier = pltpu.get_barrier_semaphore()
    peers = [(zi * NY + yi, (head + d) % NH) for d in range(1, NH)]
    peers += [(((zi + d) % NZ) * NY + yi, head) for d in (1, 2, NZ - 1, NZ - 2)]
    peers += [(zi * NY + (yi + k) % NY, head) for k in range(1, NY)]
    for peer in peers:
        pl.semaphore_signal(barrier, inc=1, device_id=peer, device_id_type=MESH)
    pl.semaphore_wait(barrier, len(peers))


def ring_routes(count, rounds):
    tables = []
    for mask in range(count):
        flows = []
        for place in range(count):
            up = (place ^ mask) - place
            up %= count
            for piece in range(2):
                if up == 0:
                    continue
                down = count - up
                forward = up < down or (up == down and piece == 0)
                flows.append(dict(at=place, left=min(up, down), step=1 if forward else -1,
                                  slot=piece, piece=piece, goal=place ^ mask))
        sends = [[[0, 0] for _ in range(rounds)] for _ in range(count)]
        final = [[0, 1] for _ in range(count)]
        for t in range(rounds):
            moved = {}
            for flow in sorted(flows, key=lambda f: (-f["left"], f["piece"], f["at"])):
                if flow["left"] == 0:
                    continue
                way = 0 if flow["step"] == 1 else 1
                if (flow["at"], way) in moved:
                    continue
                moved[flow["at"], way] = flow
            for (at, way), flow in moved.items():
                sends[at][t][way] = flow["slot"]
                flow["at"] = (at + flow["step"]) % count
                flow["left"] -= 1
                flow["slot"] = 2 + 2 * t + way
                if flow["left"] == 0:
                    assert flow["at"] == flow["goal"]
                    final[flow["at"]][flow["piece"]] = flow["slot"]
        assert all(flow["left"] == 0 for flow in flows), (count, mask)
        for place in range(count):
            tables.append([s for pair in sends[place] for s in pair] + final[place])
    return tables

ZT, YT = 4, 2
Z_ROUTES = ring_routes(NZ, ZT)
Y_ROUTES = ring_routes(NY, YT)
Z_WIDE, Y_WIDE = 2 * ZT + 2, 2 * YT + 2
STEPS = ZT + YT
HALF = BLK // 2
SPAN = GROUP * E // 2
STREAMS = ((0, 0, "zy"), (1, 0, "yz"), (0, 1, "yz"), (1, 1, "zy"))


def route_table():
    return jnp.array([v for row in Z_ROUTES + Y_ROUTES for v in row], jnp.int32)


def relay_scratch():
    count = len(STREAMS)
    dma = pltpu.SemaphoreType.DMA
    piece = (HALF, SPAN)
    return [pltpu.VMEM((count, ZT, 2) + piece, BF16), pltpu.VMEM((count, ZT, 2) + piece, BF16),
            pltpu.VMEM((count, YT, 2) + piece, BF16), pltpu.VMEM((count, YT, 2) + piece, BF16),
            pltpu.VMEM((count, 2) + piece, BF16),
            dma((count, ZT, 2)), dma((count, ZT, 2)), dma((count, YT, 2)), dma((count, YT, 2))]


RELAY_REFS = 9


class Relay:
    def __init__(self, mask_ref, table_ref, src_ref, dst_ref, scratch, place_of):
        zi, yi, head = place_of
        z_stage, z_land, y_stage, y_land, self.mid, zs, zr, ys, yr = scratch
        self.src, self.dst = src_ref, dst_ref
        self.copies = []
        self.rings = []
        self.plan = []
        for n, (r, _, order) in enumerate(STREAMS):
            mask = mask_ref[r]
            z_base = ((mask // NY) * NZ + zi) * Z_WIDE
            y_base = NZ * NZ * Z_WIDE + ((mask % NY) * NY + yi) * Y_WIDE
            rings = dict(
                z=dict(rounds=ZT, stage=z_stage, land=z_land, routes=Z_ROUTES, send=zs, recv=zr,
                       pick=[table_ref[z_base + i] for i in range(Z_WIDE)],
                       to=[(((zi + step) % NZ) * NY + yi, head) for step in (1, NZ - 1)]),
                y=dict(rounds=YT, stage=y_stage, land=y_land, routes=Y_ROUTES, send=ys, recv=yr,
                       pick=[table_ref[y_base + i] for i in range(Y_WIDE)],
                       to=[(zi * NY + (yi + step) % NY, head) for step in (1, NY - 1)]))
            self.rings.append([rings[axis] for axis in order])
            self.plan.append([(which, t) for which in range(2)
                              for t in range(self.rings[n][which]["rounds"])])

    def region(self, n, piece):
        r, part, _ = STREAMS[n]
        return pl.ds(r * BLK + piece * HALF, HALF), pl.ds(part * SPAN, SPAN)

    def value(self, n, which, slot):
        ring = self.rings[n][which]
        if slot >= 2:
            return ring["land"][n, (slot - 2) // 2, slot % 2]
        if which == 0:
            return self.src[self.region(n, slot)]
        return self.mid[n, slot]

    def choose(self, n, which, index):
        ring = self.rings[n][which]
        slots = sorted({row[index] for row in ring["routes"]})
        chosen = self.value(n, which, slots[0])
        for slot in slots[1:]:
            chosen = jnp.where(ring["pick"][index] == slot, self.value(n, which, slot), chosen)
        return chosen

    def close(self, n, which):
        ring = self.rings[n][which]
        for copy in ring["last"]:
            copy.wait_recv()
        for piece in range(2):
            chosen = self.choose(n, which, 2 * ring["rounds"] + piece)
            if which == 0:
                self.mid[n, piece] = chosen
            else:
                self.dst[self.region(n, piece)] = chosen

    def step(self, r, k):
        for n in range(len(STREAMS)):
            if STREAMS[n][0] != r:
                continue
            which, t = self.plan[n][k]
            ring = self.rings[n][which]
            if t > 0:
                for copy in ring["last"]:
                    copy.wait_recv()
            elif which == 1:
                self.close(n, 0)
            ring["last"] = []
            for way in range(2):
                ring["stage"][n, t, way] = self.choose(n, which, 2 * t + way)
            for way in range(2):
                copy = remote(ring["stage"].at[n, t, way], ring["land"].at[n, t, way],
                              ring["send"].at[n, t, way], ring["recv"].at[n, t, way], *ring["to"][way])
                copy.start()
                ring["last"].append(copy)
                self.copies.append(copy)

    def finish(self, r):
        for n in range(len(STREAMS)):
            if STREAMS[n][0] == r:
                self.close(n, 1)

    def drain(self):
        for copy in self.copies:
            copy.wait_send()


def build_keep(bits_ref, keep_ref):
    row = lax.broadcasted_iota(jnp.int32, (32, BLK), 0)
    for h in range(GROUP):
        parts = []
        for w in range(4):
            words = jnp.broadcast_to(bits_ref[h, w:w + 1, :], (32, BLK))
            parts.append((lax.shift_right_logical(words, row) & 1).astype(F32))
        kept = jnp.concatenate(parts, axis=0).T
        keep_ref[h, 0:BLK] = kept
        keep_ref[h, BLK:2 * BLK] = kept


def dot_nt(a, b):
    return lax.dot_general(a, b, (((1,), (1,)), ((), ())), preferred_element_type=F32)


def dot_nn(a, b):
    return lax.dot_general(a, b, (((1,), (0,)), ((), ())), preferred_element_type=F32)


class Attention:
    def __init__(self, docs_ref, q_ref, kw_ref, vw_ref, g_ref, keep_ref, out_ref, dq_ref, dkv_ref, scratch):
        (self.s, self.w, self.qs, self.qt, self.gs, self.gt, self.acc, self.mx, self.st, self.inv,
         self.dkt, self.dvt) = scratch
        self.docs, self.q, self.g, self.keep = docs_ref, q_ref, g_ref, keep_ref
        self.kw, self.vw = kw_ref, vw_ref
        self.out, self.dq, self.dkv = out_ref, dq_ref, dkv_ref
        self.first = 2 * lax.axis_index("ctx") - 16

    def part(self, r, j, left):
        ref = self.kw if left else self.vw
        if r == 1:
            return ref[j + 1]
        return jnp.concatenate([ref[j, BLK:2 * BLK, :], ref[j + 1, 0:BLK, :]], axis=0)

    def columns(self, r, j):
        return pl.ds(pl.multiple_of((1 + r) * BLK + j * 2 * BLK, BLK), 2 * BLK)

    def setup(self, r):
        rows = pl.ds(r * BLK, BLK)
        for h in range(GROUP):
            part = self.q[rows, pl.ds(h * E, E)]
            self.qs[r, pl.ds(h * BLK, BLK), :] = part
            self.qt[r, :, pl.ds(h * BLK, BLK)] = part.T
        self.mx[r] = jnp.full_like(self.mx[r], -jnp.inf)

    def scores(self, r, begin, end):
        lane = lax.broadcasted_iota(jnp.int32, (BLK, BLK), 1)
        row = lax.broadcasted_iota(jnp.int32, (BLK, BLK), 0)
        causal = jnp.where(lane <= row, 0.0, -jnp.inf).astype(F32)
        lane2 = lax.broadcasted_iota(jnp.int32, (1, 2 * BLK), 1)
        document = self.docs[self.first + 16 + r]
        low = 16 + r
        for w in range(1 + r, 16 + r):
            there = jnp.maximum(self.first + w, 0)
            same = jnp.where(self.docs[there] == document, 1, 0)
            low = low - jnp.where(self.first + w >= 0, same, 0)

        def score_step(j, extra):
            s = dot_nt(self.qs[r], self.part(r, j, True))
            block = (1 + r) + 2 * j + lane2 // BLK
            bias = jnp.where(block >= low, 0.0, -jnp.inf).astype(F32)
            for h in range(GROUP):
                part = s[h * BLK:(h + 1) * BLK] + bias
                left, right = part[:, :BLK], part[:, BLK:]
                if extra:
                    right = right + causal
                hr = pl.ds(h * BLK, BLK)
                self.s[r, j, hr, 0:BLK] = left
                self.s[r, j, hr, BLK:2 * BLK] = right
                self.mx[r, hr, :] = jnp.maximum(self.mx[r, hr, :], jnp.maximum(left, right))

        def score_body(j, c):
            score_step(j, False)
            return c
        lax.fori_loop(begin, min(end, PAIRS - 1), score_body, 0)
        if end == PAIRS:
            score_step(PAIRS - 1, True)

    def weigh(self, r):
        expo = math.log2(math.e) / math.sqrt(E)
        scale = 1.0 / 0.9
        rows = pl.ds(r * BLK, BLK)
        for h in range(GROUP):
            hr = pl.ds(h * BLK, BLK)
            top = jnp.max(self.mx[r, hr, :], axis=1, keepdims=True)
            self.st[hr, :] = jnp.broadcast_to(top, (BLK, BLK))
        self.mx[r] = jnp.zeros_like(self.mx[r])
        self.acc[...] = jnp.zeros_like(self.acc)

        def out_body(j, c):
            kb = self.table_row(r, j)
            for h in range(GROUP):
                hr = pl.ds(h * BLK, BLK)
                top = self.st[hr, :]
                left = jnp.exp2((self.s[r, j, hr, 0:BLK] - top) * expo)
                right = jnp.exp2((self.s[r, j, hr, BLK:2 * BLK] - top) * expo)
                self.s[r, j, hr, 0:BLK] = left
                self.s[r, j, hr, BLK:2 * BLK] = right
                self.mx[r, hr, :] = self.mx[r, hr, :] + (left + right)
                self.w[r, j, hr, 0:BLK] = (left * self.keep[h, pl.ds(kb, BLK), :]).astype(BF16)
                self.w[r, j, hr, BLK:2 * BLK] = (right * self.keep[h, pl.ds(kb + 1, BLK), :]).astype(BF16)
            self.acc[...] += dot_nn(self.w[r, j], self.part(r, j, False))
            return c
        lax.fori_loop(0, PAIRS, out_body, 0)

        for h in range(GROUP):
            hr = pl.ds(h * BLK, BLK)
            total = jnp.sum(self.mx[r, hr, :], axis=1, keepdims=True)
            inverse = 1.0 / total
            self.out[rows, pl.ds(h * E, E)] = (self.acc[hr, :] * (inverse * scale)).astype(BF16)
            self.inv[r, hr, :] = jnp.broadcast_to(inverse, (BLK, BLK))

    def table_row(self, r, j):
        kb = self.first + (1 + r) + 2 * j
        return jnp.where(kb < 0, BLK - 1, kb)

    def prepare(self, r):
        scale = 1.0 / 0.9
        rows = pl.ds(r * BLK, BLK)
        for h in range(GROUP):
            hr = pl.ds(h * BLK, BLK)
            cols = pl.ds(h * E, E)
            inverse = self.inv[r, hr, :]
            grad = self.g[rows, cols].astype(F32)
            delta = jnp.sum(grad * self.out[rows, cols].astype(F32), axis=1, keepdims=True)
            self.st[hr, :] = delta * inverse
            scaled = (grad * (inverse * scale)).astype(BF16)
            self.gs[hr, :] = scaled
            self.gt[:, hr] = scaled.T
        self.acc[...] = jnp.zeros_like(self.acc)

    def backward(self, r, begin, end):
        def grad_body(j, c):
            kb = self.table_row(r, j)
            dw = dot_nt(self.gs[...], self.part(r, j, False))
            self.dvt[:, self.columns(r, j)] += dot_nn(self.gt[...], self.w[r, j])
            for h in range(GROUP):
                hr = pl.ds(h * BLK, BLK)
                delta = self.st[hr, :]
                part = dw[h * BLK:(h + 1) * BLK]
                left = self.s[r, j, hr, 0:BLK] * (part[:, :BLK] * self.keep[h, pl.ds(kb, BLK), :] - delta)
                right = self.s[r, j, hr, BLK:2 * BLK] * (
                    part[:, BLK:] * self.keep[h, pl.ds(kb + 1, BLK), :] - delta)
                self.w[r, j, hr, 0:BLK] = left.astype(BF16)
                self.w[r, j, hr, BLK:2 * BLK] = right.astype(BF16)
            self.acc[...] += dot_nn(self.w[r, j], self.part(r, j, True))
            self.dkt[:, self.columns(r, j)] += dot_nn(self.qt[r], self.w[r, j])
            return c
        lax.fori_loop(begin, end, grad_body, 0)

    def store_query_grad(self, r):
        for h in range(GROUP):
            hr = pl.ds(h * BLK, BLK)
            self.dq[pl.ds(r * BLK, BLK), pl.ds(h * E, E)] = (self.acc[hr, :] * (1.0 / math.sqrt(E))).astype(BF16)

    def store_slot(self, slot):
        cs = pl.ds(slot * 2 * BLK, 2 * BLK)
        self.dkv[slot, :, 0:E] = (self.dkt[:, cs] * (1.0 / math.sqrt(E))).T.astype(BF16)
        self.dkv[slot, :, E:2 * E] = self.dvt[:, cs].T.astype(BF16)


def attn_scratch():
    rows = GROUP * BLK
    return [pltpu.VMEM((2, PAIRS, rows, 2 * BLK), F32),
            pltpu.VMEM((2, PAIRS, rows, 2 * BLK), BF16),
            pltpu.VMEM((2, rows, E), BF16),
            pltpu.VMEM((2, E, rows), BF16),
            pltpu.VMEM((rows, E), BF16),
            pltpu.VMEM((E, rows), BF16),
            pltpu.VMEM((rows, E), F32),
            pltpu.VMEM((2, rows, BLK), F32),
            pltpu.VMEM((rows, BLK), F32),
            pltpu.VMEM((2, rows, BLK), F32),
            pltpu.VMEM((E, WIN), F32),
            pltpu.VMEM((E, WIN), F32)]


def whole_kernel(docs_ref, mask_ref, table_ref, q_ref, k_ref, v_ref, g_ref, bits_ref,
                 ob_ref, gq_ref, gk_ref, gv_ref,
                 qb_ref, kw_ref, vw_ref, gb_ref, keep_ref, out_ref, dq_ref, dkv_ref,
                 r_ref, zs_ref, zr_ref, own_ref, fin_ref,
                 kv_send, kv_recv, q_send, q_recv, z_send, z_recv, y_send, y_recv, own_sem,
                 dkv_send, dkv_recv, dq_send, dq_recv, dz_send, dz_recv, dy_send, dy_recv, down_sem,
                 *scratch):
    zi, yi, head = place()
    ctx = zi * NY + yi
    spot = (zi, yi, head)
    grad_move = Relay(mask_ref, table_ref, g_ref, gb_ref, scratch[:RELAY_REFS], spot)
    out_move = Relay(mask_ref, table_ref, out_ref, ob_ref, scratch[RELAY_REFS:2 * RELAY_REFS], spot)
    attn = Attention(docs_ref, qb_ref, kw_ref, vw_ref, gb_ref, keep_ref, out_ref, dq_ref, dkv_ref,
                     scratch[2 * RELAY_REFS:])
    mine = pl.ds(pl.multiple_of(head * 32, 32), 32)
    wide = pl.ds(pl.multiple_of(head * GROUP * E, GROUP * E), GROUP * E)
    slim = pl.ds(pl.multiple_of(head * E, E), E)
    greet(zi, yi, head)

    own = [
        pltpu.make_async_copy(k_ref.at[:, slim], kw_ref.at[8, mine, :], own_sem.at[0]),
        pltpu.make_async_copy(v_ref.at[:, slim], vw_ref.at[8, mine, :], own_sem.at[1]),
        pltpu.make_async_copy(q_ref.at[:, wide], qb_ref.at[mine, :], own_sem.at[2]),
    ]
    for copy in own:
        copy.start()
    windows = (kw_ref, vw_ref)
    kv_copies = [[], []]
    for kind, ref in enumerate((k_ref, v_ref)):
        for d in range(1, NH):
            to = (head + d) % NH
            cols = pl.ds(pl.multiple_of(to * E, E), E)
            copy = remote(ref.at[:, cols], windows[kind].at[8, mine, :],
                          kv_send.at[kind, d], kv_recv.at[kind, d], ctx, to)
            copy.start()
            kv_copies[kind].append(copy)
    q_copies = []
    for d in range(1, NH):
        to = (head + d) % NH
        cols = pl.ds(pl.multiple_of(to * GROUP * E, GROUP * E), GROUP * E)
        copy = remote(q_ref.at[:, cols], qb_ref.at[mine, :], q_send.at[d], q_recv.at[d], ctx, to)
        copy.start()
        q_copies.append(copy)
    grad_move.step(0, 0)
    grad_move.step(1, 0)
    build_keep(bits_ref, keep_ref)
    attn.dkt[...] = jnp.zeros_like(attn.dkt)
    attn.dvt[...] = jnp.zeros_like(attn.dvt)
    z_copies = [[], []]
    y_copies = [[], []]
    for kind, win in enumerate(windows):
        own[kind].wait()
        for copy in kv_copies[kind]:
            copy.wait_recv()
        for d in (1, 2):
            copy = remote(win.at[8], win.at[8 - 4 * d], z_send.at[kind, d], z_recv.at[kind, d],
                          ((zi + d) % NZ) * NY + yi, head)
            copy.start()
            z_copies[kind].append(copy)
        for part in range(2):
            for k in range(1, NY):
                wrap = (yi + k) // NY
                y_copies[kind].append((part, wrap, remote(
                    win.at[8 - 4 * part - 4 * wrap], win.at[8 - 4 * part - k],
                    y_send.at[kind, part, k], y_recv.at[kind, part, k], zi * NY + (yi + k) % NY, head)))
        for part, wrap, copy in y_copies[kind]:
            if part == 0:
                @pl.when(wrap == 0)
                def _(copy=copy):
                    copy.start()
    grad_move.step(0, 1)
    for kind in range(2):
        z_copies[kind][0].wait_recv()
        for part, wrap, copy in y_copies[kind]:
            @pl.when(wrap == 1 - part)
            def _(copy=copy):
                copy.start()
        z_copies[kind][1].wait_recv()
        for part, wrap, copy in y_copies[kind]:
            if part == 1:
                @pl.when(wrap == 1)
                def _(copy=copy):
                    copy.start()
        grad_move.step(kind, 2 - kind)
    grad_move.step(0, 3)
    for copy in q_copies:
        copy.wait_recv()
    own[2].wait()
    attn.setup(0)
    attn.setup(1)
    for part, _, copy in y_copies[0]:
        if part == 0:
            copy.wait_recv()
    attn.scores(0, PAIRS // 2, PAIRS)
    attn.scores(1, PAIRS // 2, PAIRS)
    grad_move.step(0, 4)
    grad_move.step(1, 2)
    for part, _, copy in y_copies[0]:
        if part == 1:
            copy.wait_recv()
    attn.scores(0, 0, PAIRS // 2)
    attn.scores(1, 0, PAIRS // 2)
    grad_move.step(0, 5)
    grad_move.step(1, 3)
    for _, _, copy in y_copies[1]:
        copy.wait_recv()
    attn.weigh(0)
    out_move.step(0, 0)
    grad_move.step(1, 4)
    attn.weigh(1)
    out_move.step(1, 0)
    grad_move.step(1, 5)
    grad_move.finish(0)

    dq_copies = []

    def send_query_grads(r):
        for d in range(1, NH):
            to = (head + d) % NH
            rows = pl.ds(pl.multiple_of(to * 32, 32), 32)
            copy = remote(dq_ref.at[rows, :], gq_ref.at[:, wide], dq_send.at[d], dq_recv.at[d], ctx, to)
            if r == 0:
                dq_copies.append(copy)

            @pl.when(to // (NH // 2) == r)
            def _(copy=copy):
                copy.start()

    dy_copies = []

    def send_slots(part):
        for k in range(1, NY):
            slot = 8 - 4 * part - k
            attn.store_slot(slot)
            copy = remote(dkv_ref.at[slot], r_ref.at[part, k - 1],
                          dy_send.at[part, k], dy_recv.at[part, k], zi * NY + (yi + NY - k) % NY, head)
            copy.start()
            dy_copies.append(copy)

    attn.prepare(0)
    attn.backward(0, 0, 3)
    out_move.step(0, 1)
    out_move.step(1, 1)
    attn.backward(0, 3, 6)
    out_move.step(0, 2)
    grad_move.finish(1)
    attn.backward(0, 6, PAIRS)
    attn.store_query_grad(0)
    send_query_grads(0)
    attn.store_slot(0)
    out_move.step(1, 2)
    attn.prepare(1)
    attn.backward(1, 0, 3)
    send_slots(1)
    out_move.step(0, 3)
    out_move.step(1, 3)
    attn.backward(1, 3, 5)
    out_move.step(0, 4)
    attn.backward(1, 5, 7)
    send_slots(0)
    for copy in dy_copies[:NY - 1]:
        copy.wait_recv()
    wraps = [(yi + k) // NY > 0 for k in range(NY)]
    total = dkv_ref[0].astype(F32)
    for k in range(1, NY):
        second = r_ref[1, k - 1].astype(F32)
        total = total + jnp.where(wraps[k], second, jnp.zeros_like(second))
    zs_ref[1] = total.astype(BF16)
    dz_copies = []

    def send_plane(d):
        copy = remote(zs_ref.at[d - 1], zr_ref.at[d - 1], dz_send.at[d], dz_recv.at[d],
                      ((zi + NZ - d) % NZ) * NY + yi, head)
        copy.start()
        dz_copies.append(copy)

    send_plane(2)
    out_move.step(1, 4)
    attn.backward(1, 7, 8)
    attn.store_query_grad(1)
    send_query_grads(1)
    for slot in (4, 8):
        attn.store_slot(slot)
    down = [pltpu.make_async_copy(dq_ref.at[mine, :], gq_ref.at[:, wide], down_sem.at[0])]
    down[0].start()
    for copy in dy_copies[NY - 1:]:
        copy.wait_recv()
    total = dkv_ref[4].astype(F32)
    keep_here = dkv_ref[8].astype(F32)
    for k in range(1, NY):
        first, second = r_ref[0, k - 1].astype(F32), r_ref[1, k - 1].astype(F32)
        total = total + jnp.where(wraps[k], first, second)
        keep_here = keep_here + jnp.where(wraps[k], jnp.zeros_like(first), first)
    zs_ref[0] = total.astype(BF16)
    own_ref[...] = keep_here
    send_plane(1)
    out_move.step(0, 5)
    out_move.step(1, 5)
    for copy in dz_copies:
        copy.wait_recv()
    fin_ref[...] = (own_ref[...] + zr_ref[0].astype(F32) + zr_ref[1].astype(F32)).astype(BF16)
    dkv_copies = []
    for d in range(1, NH):
        to = (head + d) % NH
        rows = pl.ds(pl.multiple_of(to * 32, 32), 32)
        for part, ref in enumerate((gk_ref, gv_ref)):
            copy = remote(fin_ref.at[rows, pl.ds(part * E, E)], ref.at[:, slim],
                          dkv_send.at[part, d], dkv_recv.at[part, d], ctx, to)
            copy.start()
            dkv_copies.append(copy)
    for part, ref in enumerate((gk_ref, gv_ref)):
        copy = pltpu.make_async_copy(fin_ref.at[mine, pl.ds(part * E, E)], ref.at[:, slim],
                                     down_sem.at[1 + part])
        copy.start()
        down.append(copy)
    out_move.finish(0)
    out_move.finish(1)
    for copy in dq_copies + dkv_copies:
        copy.wait_recv()
    for copy in down:
        copy.wait()
    grad_move.drain()
    out_move.drain()
    for copy in q_copies + dq_copies + dkv_copies + dy_copies + dz_copies:
        copy.wait_send()
    for kind in range(2):
        for copy in kv_copies[kind] + z_copies[kind]:
            copy.wait_send()
        for _, _, copy in y_copies[kind]:
            copy.wait_send()


def settle_kernel(*refs):
    for src, dst in zip(refs[:4], refs[4:]):
        dst[...] = src[...]


def on_device(query, key, value, grad_out, doc_ids, relay_mask, drop_bits):
    vm = pl.BlockSpec(memory_space=pltpu.VMEM)
    sm = pl.BlockSpec(memory_space=pltpu.SMEM)
    dma = pltpu.SemaphoreType.DMA
    heads = [dma((2, NH)), dma((2, NH)), dma((NH,)), dma((NH,))]
    up = heads + [dma((2, 3)), dma((2, 3)), dma((2, 2, NY)), dma((2, 2, NY)), dma((3,))]
    down = heads + [dma((3,)), dma((3,)), dma((2, NY)), dma((2, NY)), dma((3,))]
    shapes = (jax.ShapeDtypeStruct((2 * BLK, GROUP * E), BF16),
                   jax.ShapeDtypeStruct((32, NH * GROUP * E), BF16),
                   jax.ShapeDtypeStruct((32, NH * E), BF16),
                   jax.ShapeDtypeStruct((32, NH * E), BF16))
    results = pl.pallas_call(
        whole_kernel,
        out_shape=shapes,
        in_specs=[sm, sm, sm, vm, vm, vm, vm, vm],
        out_specs=(vm, vm, vm, vm),
        scratch_shapes=[
            pltpu.VMEM((2 * BLK, GROUP * E), BF16),
            pltpu.VMEM((9, 2 * BLK, E), BF16),
            pltpu.VMEM((9, 2 * BLK, E), BF16),
            pltpu.VMEM((2 * BLK, GROUP * E), BF16),
            pltpu.VMEM((GROUP, 2 * BLK, BLK), F32),
            pltpu.VMEM((2 * BLK, GROUP * E), BF16),
            pltpu.VMEM((2 * BLK, GROUP * E), BF16),
            pltpu.VMEM((9, 2 * BLK, 2 * E), BF16),
            pltpu.VMEM((2, NY - 1, 2 * BLK, 2 * E), BF16),
            pltpu.VMEM((2, 2 * BLK, 2 * E), BF16),
            pltpu.VMEM((2, 2 * BLK, 2 * E), BF16),
            pltpu.VMEM((2 * BLK, 2 * E), F32),
            pltpu.VMEM((2 * BLK, 2 * E), BF16),
        ] + up + down + relay_scratch() + relay_scratch() + attn_scratch(),
        compiler_params=pltpu.CompilerParams(
            collective_id=0, has_side_effects=True, vmem_limit_bytes=60 * 1024 * 1024),
    )(doc_ids, relay_mask, route_table(), query, key, value, grad_out, drop_bits.transpose(0, 2, 1))
    return pl.pallas_call(
        settle_kernel, out_shape=shapes, in_specs=[vm] * 4, out_specs=(vm,) * 4)(*results)


def solution(mesh):
    placed = (
        P(("ctx", "head"), None),
        P(("ctx", "head"), None),
        P(("ctx", "head"), None),
        P("ctx", "head"),
        P(),
        P(),
        P("head", None, None),
    )
    return jax.shard_map(
        on_device,
        mesh=mesh,
        in_specs=placed,
        out_specs=(
            P("ctx", "head"),
            P(("ctx", "head"), None),
            P(("ctx", "head"), None),
            P(("ctx", "head"), None),
        ),
        check_vma=False,
    )
```

```python
import math

import jax
import jax.numpy as jnp
from jax import lax
from jax.experimental import pallas as pl
from jax.experimental.pallas import tpu as pltpu
from jax.sharding import PartitionSpec as P

E = 128
BLK = 128
GROUP = 8
PAIRS = 8
WIN = 18 * BLK
NZ, NY, NH = 8, 4, 8
F32 = jnp.float32
BF16 = jnp.bfloat16
MESH = pl.DeviceIdType.MESH


def place():
    ctx, head = lax.axis_index("ctx"), lax.axis_index("head")
    return ctx // NY, ctx % NY, head


def remote(src, dst, send, recv, ctx, head):
    return pltpu.make_async_remote_copy(
        src_ref=src, dst_ref=dst, send_sem=send, recv_sem=recv,
        device_id=(ctx, head), device_id_type=MESH)


def greet(zi, yi, head):
    barrier = pltpu.get_barrier_semaphore()
    peers = [(zi * NY + yi, (head + d) % NH) for d in range(1, NH)]
    peers += [(((zi + d) % NZ) * NY + yi, head) for d in (1, 2, NZ - 1, NZ - 2)]
    peers += [(zi * NY + (yi + k) % NY, head) for k in range(1, NY)]
    for peer in peers:
        pl.semaphore_signal(barrier, inc=1, device_id=peer, device_id_type=MESH)
    pl.semaphore_wait(barrier, len(peers))


def ring_routes(count, rounds):
    tables = []
    for mask in range(count):
        flows = []
        for place in range(count):
            up = (place ^ mask) - place
            up %= count
            for piece in range(2):
                if up == 0:
                    continue
                down = count - up
                forward = up < down or (up == down and piece == 0)
                flows.append(dict(at=place, left=min(up, down), step=1 if forward else -1,
                                  slot=piece, piece=piece, goal=place ^ mask))
        sends = [[[0, 0] for _ in range(rounds)] for _ in range(count)]
        final = [[0, 1] for _ in range(count)]
        for t in range(rounds):
            moved = {}
            for flow in sorted(flows, key=lambda f: (-f["left"], f["piece"], f["at"])):
                if flow["left"] == 0:
                    continue
                way = 0 if flow["step"] == 1 else 1
                if (flow["at"], way) in moved:
                    continue
                moved[flow["at"], way] = flow
            for (at, way), flow in moved.items():
                sends[at][t][way] = flow["slot"]
                flow["at"] = (at + flow["step"]) % count
                flow["left"] -= 1
                flow["slot"] = 2 + 2 * t + way
                if flow["left"] == 0:
                    assert flow["at"] == flow["goal"]
                    final[flow["at"]][flow["piece"]] = flow["slot"]
        assert all(flow["left"] == 0 for flow in flows), (count, mask)
        for place in range(count):
            tables.append([s for pair in sends[place] for s in pair] + final[place])
    return tables

ZT, YT = 4, 2
Z_ROUTES = ring_routes(NZ, ZT)
Y_ROUTES = ring_routes(NY, YT)
Z_WIDE, Y_WIDE = 2 * ZT + 2, 2 * YT + 2
STEPS = ZT + YT
HALF = BLK // 2
SPAN = GROUP * E // 2
STREAMS = ((0, 0, "zy"), (1, 0, "yz"), (0, 1, "yz"), (1, 1, "zy"))


def route_table():
    return jnp.array([v for row in Z_ROUTES + Y_ROUTES for v in row], jnp.int32)


def relay_scratch():
    count = len(STREAMS)
    dma = pltpu.SemaphoreType.DMA
    piece = (HALF, SPAN)
    return [pltpu.VMEM((count, ZT, 2) + piece, BF16), pltpu.VMEM((count, ZT, 2) + piece, BF16),
            pltpu.VMEM((count, YT, 2) + piece, BF16), pltpu.VMEM((count, YT, 2) + piece, BF16),
            pltpu.VMEM((count, 2) + piece, BF16),
            dma((count, ZT, 2)), dma((count, ZT, 2)), dma((count, YT, 2)), dma((count, YT, 2))]


RELAY_REFS = 9


class Relay:
    def __init__(self, mask_ref, table_ref, src_ref, dst_ref, scratch, place_of):
        zi, yi, head = place_of
        z_stage, z_land, y_stage, y_land, self.mid, zs, zr, ys, yr = scratch
        self.src, self.dst = src_ref, dst_ref
        self.copies = []
        self.rings = []
        self.plan = []
        for n, (r, _, order) in enumerate(STREAMS):
            mask = mask_ref[r]
            z_base = ((mask // NY) * NZ + zi) * Z_WIDE
            y_base = NZ * NZ * Z_WIDE + ((mask % NY) * NY + yi) * Y_WIDE
            rings = dict(
                z=dict(rounds=ZT, stage=z_stage, land=z_land, routes=Z_ROUTES, send=zs, recv=zr,
                       pick=[table_ref[z_base + i] for i in range(Z_WIDE)],
                       to=[(((zi + step) % NZ) * NY + yi, head) for step in (1, NZ - 1)]),
                y=dict(rounds=YT, stage=y_stage, land=y_land, routes=Y_ROUTES, send=ys, recv=yr,
                       pick=[table_ref[y_base + i] for i in range(Y_WIDE)],
                       to=[(zi * NY + (yi + step) % NY, head) for step in (1, NY - 1)]))
            self.rings.append([rings[axis] for axis in order])
            self.plan.append([(which, t) for which in range(2)
                              for t in range(self.rings[n][which]["rounds"])])

    def region(self, n, piece):
        r, part, _ = STREAMS[n]
        return pl.ds(r * BLK + piece * HALF, HALF), pl.ds(part * SPAN, SPAN)

    def value(self, n, which, slot):
        ring = self.rings[n][which]
        if slot >= 2:
            return ring["land"][n, (slot - 2) // 2, slot % 2]
        if which == 0:
            return self.src[self.region(n, slot)]
        return self.mid[n, slot]

    def choose(self, n, which, index):
        ring = self.rings[n][which]
        slots = sorted({row[index] for row in ring["routes"]})
        chosen = self.value(n, which, slots[0])
        for slot in slots[1:]:
            chosen = jnp.where(ring["pick"][index] == slot, self.value(n, which, slot), chosen)
        return chosen

    def close(self, n, which):
        ring = self.rings[n][which]
        for copy in ring["last"]:
            copy.wait_recv()
        for piece in range(2):
            chosen = self.choose(n, which, 2 * ring["rounds"] + piece)
            if which == 0:
                self.mid[n, piece] = chosen
            else:
                self.dst[self.region(n, piece)] = chosen

    def step(self, r, k):
        for n in range(len(STREAMS)):
            if STREAMS[n][0] != r:
                continue
            which, t = self.plan[n][k]
            ring = self.rings[n][which]
            if t > 0:
                for copy in ring["last"]:
                    copy.wait_recv()
            elif which == 1:
                self.close(n, 0)
            ring["last"] = []
            for way in range(2):
                ring["stage"][n, t, way] = self.choose(n, which, 2 * t + way)
            for way in range(2):
                copy = remote(ring["stage"].at[n, t, way], ring["land"].at[n, t, way],
                              ring["send"].at[n, t, way], ring["recv"].at[n, t, way], *ring["to"][way])
                copy.start()
                ring["last"].append(copy)
                self.copies.append(copy)

    def finish(self, r):
        for n in range(len(STREAMS)):
            if STREAMS[n][0] == r:
                self.close(n, 1)

    def drain(self):
        for copy in self.copies:
            copy.wait_send()


def build_keep(bits_ref, keep_ref):
    row = lax.broadcasted_iota(jnp.int32, (32, BLK), 0)
    for h in range(GROUP):
        parts = []
        for w in range(4):
            words = jnp.broadcast_to(bits_ref[h, w:w + 1, :], (32, BLK))
            parts.append((lax.shift_right_logical(words, row) & 1).astype(F32))
        kept = jnp.concatenate(parts, axis=0).T
        keep_ref[h, 0:BLK] = kept
        keep_ref[h, BLK:2 * BLK] = kept


def dot_nt(a, b):
    return lax.dot_general(a, b, (((1,), (1,)), ((), ())), preferred_element_type=F32)


def dot_nn(a, b):
    return lax.dot_general(a, b, (((1,), (0,)), ((), ())), preferred_element_type=F32)


class Attention:
    def __init__(self, docs_ref, q_ref, kw_ref, vw_ref, g_ref, keep_ref, out_ref, dq_ref, dkv_ref, scratch):
        (self.s, self.w, self.qs, self.qt, self.gs, self.gt, self.acc, self.mx, self.st, self.inv,
         self.dkt, self.dvt) = scratch
        self.docs, self.q, self.g, self.keep = docs_ref, q_ref, g_ref, keep_ref
        self.kw, self.vw = kw_ref, vw_ref
        self.out, self.dq, self.dkv = out_ref, dq_ref, dkv_ref
        self.first = 2 * lax.axis_index("ctx") - 16

    def part(self, r, j, left):
        ref = self.kw if left else self.vw
        if r == 1:
            return ref[j + 1]
        return jnp.concatenate([ref[j, BLK:2 * BLK, :], ref[j + 1, 0:BLK, :]], axis=0)

    def columns(self, r, j):
        return pl.ds(pl.multiple_of((1 + r) * BLK + j * 2 * BLK, BLK), 2 * BLK)

    def setup(self, r):
        rows = pl.ds(r * BLK, BLK)
        for h in range(GROUP):
            part = self.q[rows, pl.ds(h * E, E)]
            self.qs[r, pl.ds(h * BLK, BLK), :] = part
            self.qt[r, :, pl.ds(h * BLK, BLK)] = part.T
        self.mx[r] = jnp.full_like(self.mx[r], -jnp.inf)

    def scores(self, r, begin, end):
        lane = lax.broadcasted_iota(jnp.int32, (BLK, BLK), 1)
        row = lax.broadcasted_iota(jnp.int32, (BLK, BLK), 0)
        causal = jnp.where(lane <= row, 0.0, -jnp.inf).astype(F32)
        lane2 = lax.broadcasted_iota(jnp.int32, (1, 2 * BLK), 1)
        document = self.docs[self.first + 16 + r]
        low = 16 + r
        for w in range(1 + r, 16 + r):
            there = jnp.maximum(self.first + w, 0)
            same = jnp.where(self.docs[there] == document, 1, 0)
            low = low - jnp.where(self.first + w >= 0, same, 0)

        def score_step(j, extra):
            s = dot_nt(self.qs[r], self.part(r, j, True))
            block = (1 + r) + 2 * j + lane2 // BLK
            bias = jnp.where(block >= low, 0.0, -jnp.inf).astype(F32)
            for h in range(GROUP):
                part = s[h * BLK:(h + 1) * BLK] + bias
                left, right = part[:, :BLK], part[:, BLK:]
                if extra:
                    right = right + causal
                hr = pl.ds(h * BLK, BLK)
                self.s[r, j, hr, 0:BLK] = left
                self.s[r, j, hr, BLK:2 * BLK] = right
                self.mx[r, hr, :] = jnp.maximum(self.mx[r, hr, :], jnp.maximum(left, right))

        def score_body(j, c):
            score_step(j, False)
            return c
        lax.fori_loop(begin, min(end, PAIRS - 1), score_body, 0)
        if end == PAIRS:
            score_step(PAIRS - 1, True)

    def weigh(self, r):
        expo = math.log2(math.e) / math.sqrt(E)
        scale = 1.0 / 0.9
        rows = pl.ds(r * BLK, BLK)
        for h in range(GROUP):
            hr = pl.ds(h * BLK, BLK)
            top = jnp.max(self.mx[r, hr, :], axis=1, keepdims=True)
            self.st[hr, :] = jnp.broadcast_to(top, (BLK, BLK))
        self.mx[r] = jnp.zeros_like(self.mx[r])
        self.acc[...] = jnp.zeros_like(self.acc)

        def out_body(j, c):
            kb = self.table_row(r, j)
            for h in range(GROUP):
                hr = pl.ds(h * BLK, BLK)
                top = self.st[hr, :]
                left = jnp.exp2((self.s[r, j, hr, 0:BLK] - top) * expo)
                right = jnp.exp2((self.s[r, j, hr, BLK:2 * BLK] - top) * expo)
                self.s[r, j, hr, 0:BLK] = left
                self.s[r, j, hr, BLK:2 * BLK] = right
                self.mx[r, hr, :] = self.mx[r, hr, :] + (left + right)
                self.w[r, j, hr, 0:BLK] = (left * self.keep[h, pl.ds(kb, BLK), :]).astype(BF16)
                self.w[r, j, hr, BLK:2 * BLK] = (right * self.keep[h, pl.ds(kb + 1, BLK), :]).astype(BF16)
            self.acc[...] += dot_nn(self.w[r, j], self.part(r, j, False))
            return c
        lax.fori_loop(0, PAIRS, out_body, 0)

        for h in range(GROUP):
            hr = pl.ds(h * BLK, BLK)
            total = jnp.sum(self.mx[r, hr, :], axis=1, keepdims=True)
            inverse = 1.0 / total
            self.out[rows, pl.ds(h * E, E)] = (self.acc[hr, :] * (inverse * scale)).astype(BF16)
            self.inv[r, hr, :] = jnp.broadcast_to(inverse, (BLK, BLK))

    def table_row(self, r, j):
        kb = self.first + (1 + r) + 2 * j
        return jnp.where(kb < 0, BLK - 1, kb)

    def prepare(self, r):
        scale = 1.0 / 0.9
        rows = pl.ds(r * BLK, BLK)
        for h in range(GROUP):
            hr = pl.ds(h * BLK, BLK)
            cols = pl.ds(h * E, E)
            inverse = self.inv[r, hr, :]
            grad = self.g[rows, cols].astype(F32)
            delta = jnp.sum(grad * self.out[rows, cols].astype(F32), axis=1, keepdims=True)
            self.st[hr, :] = delta * inverse
            scaled = (grad * (inverse * scale)).astype(BF16)
            self.gs[hr, :] = scaled
            self.gt[:, hr] = scaled.T
        self.acc[...] = jnp.zeros_like(self.acc)

    def backward(self, r, begin, end):
        def grad_body(j, c):
            kb = self.table_row(r, j)
            dw = dot_nt(self.gs[...], self.part(r, j, False))
            self.dvt[:, self.columns(r, j)] += dot_nn(self.gt[...], self.w[r, j])
            for h in range(GROUP):
                hr = pl.ds(h * BLK, BLK)
                delta = self.st[hr, :]
                part = dw[h * BLK:(h + 1) * BLK]
                left = self.s[r, j, hr, 0:BLK] * (part[:, :BLK] * self.keep[h, pl.ds(kb, BLK), :] - delta)
                right = self.s[r, j, hr, BLK:2 * BLK] * (
                    part[:, BLK:] * self.keep[h, pl.ds(kb + 1, BLK), :] - delta)
                self.w[r, j, hr, 0:BLK] = left.astype(BF16)
                self.w[r, j, hr, BLK:2 * BLK] = right.astype(BF16)
            self.acc[...] += dot_nn(self.w[r, j], self.part(r, j, True))
            self.dkt[:, self.columns(r, j)] += dot_nn(self.qt[r], self.w[r, j])
            return c
        lax.fori_loop(begin, end, grad_body, 0)

    def store_query_grad(self, r):
        for h in range(GROUP):
            hr = pl.ds(h * BLK, BLK)
            self.dq[pl.ds(r * BLK, BLK), pl.ds(h * E, E)] = (self.acc[hr, :] * (1.0 / math.sqrt(E))).astype(BF16)

    def store_slot(self, slot):
        cs = pl.ds(slot * 2 * BLK, 2 * BLK)
        self.dkv[slot, :, 0:E] = (self.dkt[:, cs] * (1.0 / math.sqrt(E))).T.astype(BF16)
        self.dkv[slot, :, E:2 * E] = self.dvt[:, cs].T.astype(BF16)


def attn_scratch():
    rows = GROUP * BLK
    return [pltpu.VMEM((2, PAIRS, rows, 2 * BLK), F32),
            pltpu.VMEM((2, PAIRS, rows, 2 * BLK), BF16),
            pltpu.VMEM((2, rows, E), BF16),
            pltpu.VMEM((2, E, rows), BF16),
            pltpu.VMEM((rows, E), BF16),
            pltpu.VMEM((E, rows), BF16),
            pltpu.VMEM((rows, E), F32),
            pltpu.VMEM((2, rows, BLK), F32),
            pltpu.VMEM((rows, BLK), F32),
            pltpu.VMEM((2, rows, BLK), F32),
            pltpu.VMEM((E, WIN), F32),
            pltpu.VMEM((E, WIN), F32)]


def whole_kernel(docs_ref, mask_ref, table_ref, q_ref, k_ref, v_ref, g_ref, bits_ref,
                 ob_ref, gq_ref, gk_ref, gv_ref,
                 qb_ref, kw_ref, vw_ref, gb_ref, keep_ref, out_ref, dq_ref, dkv_ref,
                 r_ref, zs_ref, zr_ref, own_ref, fin_ref,
                 kv_send, kv_recv, q_send, q_recv, z_send, z_recv, y_send, y_recv, own_sem,
                 dkv_send, dkv_recv, dq_send, dq_recv, dz_send, dz_recv, dy_send, dy_recv, down_sem,
                 *scratch):
    zi, yi, head = place()
    ctx = zi * NY + yi
    spot = (zi, yi, head)
    grad_move = Relay(mask_ref, table_ref, g_ref, gb_ref, scratch[:RELAY_REFS], spot)
    out_move = Relay(mask_ref, table_ref, out_ref, ob_ref, scratch[RELAY_REFS:2 * RELAY_REFS], spot)
    attn = Attention(docs_ref, qb_ref, kw_ref, vw_ref, gb_ref, keep_ref, out_ref, dq_ref, dkv_ref,
                     scratch[2 * RELAY_REFS:])
    mine = pl.ds(pl.multiple_of(head * 32, 32), 32)
    wide = pl.ds(pl.multiple_of(head * GROUP * E, GROUP * E), GROUP * E)
    slim = pl.ds(pl.multiple_of(head * E, E), E)
    greet(zi, yi, head)

    own = [
        pltpu.make_async_copy(k_ref.at[:, slim], kw_ref.at[8, mine, :], own_sem.at[0]),
        pltpu.make_async_copy(v_ref.at[:, slim], vw_ref.at[8, mine, :], own_sem.at[1]),
        pltpu.make_async_copy(q_ref.at[:, wide], qb_ref.at[mine, :], own_sem.at[2]),
    ]
    for copy in own:
        copy.start()
    windows = (kw_ref, vw_ref)
    kv_copies = [[], []]
    for kind, ref in enumerate((k_ref, v_ref)):
        for d in range(1, NH):
            to = (head + d) % NH
            cols = pl.ds(pl.multiple_of(to * E, E), E)
            copy = remote(ref.at[:, cols], windows[kind].at[8, mine, :],
                          kv_send.at[kind, d], kv_recv.at[kind, d], ctx, to)
            copy.start()
            kv_copies[kind].append(copy)
    q_copies = []
    for d in range(1, NH):
        to = (head + d) % NH
        cols = pl.ds(pl.multiple_of(to * GROUP * E, GROUP * E), GROUP * E)
        copy = remote(q_ref.at[:, cols], qb_ref.at[mine, :], q_send.at[d], q_recv.at[d], ctx, to)
        copy.start()
        q_copies.append(copy)
    grad_move.step(0, 0)
    grad_move.step(1, 0)
    build_keep(bits_ref, keep_ref)
    attn.dkt[...] = jnp.zeros_like(attn.dkt)
    attn.dvt[...] = jnp.zeros_like(attn.dvt)
    z_copies = [[], []]
    y_copies = [[], []]
    for kind, win in enumerate(windows):
        own[kind].wait()
        for copy in kv_copies[kind]:
            copy.wait_recv()
        for d in (1, 2):
            copy = remote(win.at[8], win.at[8 - 4 * d], z_send.at[kind, d], z_recv.at[kind, d],
                          ((zi + d) % NZ) * NY + yi, head)
            copy.start()
            z_copies[kind].append(copy)
        for part in range(2):
            for k in range(1, NY):
                wrap = (yi + k) // NY
                y_copies[kind].append((part, wrap, remote(
                    win.at[8 - 4 * part - 4 * wrap], win.at[8 - 4 * part - k],
                    y_send.at[kind, part, k], y_recv.at[kind, part, k], zi * NY + (yi + k) % NY, head)))
        for part, wrap, copy in y_copies[kind]:
            if part == 0:
                @pl.when(wrap == 0)
                def _(copy=copy):
                    copy.start()
    grad_move.step(0, 1)
    for kind in range(2):
        z_copies[kind][0].wait_recv()
        for part, wrap, copy in y_copies[kind]:
            @pl.when(wrap == 1 - part)
            def _(copy=copy):
                copy.start()
        z_copies[kind][1].wait_recv()
        for part, wrap, copy in y_copies[kind]:
            if part == 1:
                @pl.when(wrap == 1)
                def _(copy=copy):
                    copy.start()
    grad_move.step(0, 2)
    grad_move.step(1, 1)
    for copy in q_copies:
        copy.wait_recv()
    own[2].wait()
    attn.setup(0)
    attn.setup(1)
    for part, _, copy in y_copies[0]:
        if part == 0:
            copy.wait_recv()
    attn.scores(0, PAIRS // 2, PAIRS)
    attn.scores(1, PAIRS // 2, PAIRS)
    grad_move.step(0, 3)
    grad_move.step(1, 2)
    for part, _, copy in y_copies[0]:
        if part == 1:
            copy.wait_recv()
    attn.scores(0, 0, PAIRS // 2)
    attn.scores(1, 0, PAIRS // 2)
    grad_move.step(0, 4)
    grad_move.step(1, 3)
    for _, _, copy in y_copies[1]:
        copy.wait_recv()
    attn.weigh(0)
    out_move.step(0, 0)
    grad_move.step(0, 5)
    grad_move.step(1, 4)
    attn.weigh(1)
    out_move.step(1, 0)
    grad_move.step(1, 5)
    grad_move.finish(0)

    dq_copies = []

    def send_query_grads(r):
        for d in range(1, NH):
            to = (head + d) % NH
            rows = pl.ds(pl.multiple_of(to * 32, 32), 32)
            copy = remote(dq_ref.at[rows, :], gq_ref.at[:, wide], dq_send.at[d], dq_recv.at[d], ctx, to)
            if r == 0:
                dq_copies.append(copy)

            @pl.when(to // (NH // 2) == r)
            def _(copy=copy):
                copy.start()

    dy_copies = []

    def send_slots(part):
        for k in range(1, NY):
            slot = 8 - 4 * part - k
            attn.store_slot(slot)
            copy = remote(dkv_ref.at[slot], r_ref.at[part, k - 1],
                          dy_send.at[part, k], dy_recv.at[part, k], zi * NY + (yi + NY - k) % NY, head)
            copy.start()
            dy_copies.append(copy)

    attn.prepare(0)
    attn.backward(0, 0, 3)
    out_move.step(0, 1)
    out_move.step(1, 1)
    attn.backward(0, 3, 6)
    out_move.step(0, 2)
    grad_move.finish(1)
    attn.backward(0, 6, PAIRS)
    attn.store_query_grad(0)
    send_query_grads(0)
    attn.store_slot(0)
    out_move.step(1, 2)
    attn.prepare(1)
    attn.backward(1, 0, 3)
    send_slots(1)
    out_move.step(0, 3)
    out_move.step(1, 3)
    attn.backward(1, 3, 5)
    out_move.step(0, 4)
    attn.backward(1, 5, 7)
    send_slots(0)
    for copy in dy_copies[:NY - 1]:
        copy.wait_recv()
    wraps = [(yi + k) // NY > 0 for k in range(NY)]
    total = dkv_ref[0].astype(F32)
    for k in range(1, NY):
        second = r_ref[1, k - 1].astype(F32)
        total = total + jnp.where(wraps[k], second, jnp.zeros_like(second))
    zs_ref[1] = total.astype(BF16)
    dz_copies = []

    def send_plane(d):
        copy = remote(zs_ref.at[d - 1], zr_ref.at[d - 1], dz_send.at[d], dz_recv.at[d],
                      ((zi + NZ - d) % NZ) * NY + yi, head)
        copy.start()
        dz_copies.append(copy)

    send_plane(2)
    out_move.step(1, 4)
    attn.backward(1, 7, 8)
    attn.store_query_grad(1)
    send_query_grads(1)
    for slot in (4, 8):
        attn.store_slot(slot)
    down = [pltpu.make_async_copy(dq_ref.at[mine, :], gq_ref.at[:, wide], down_sem.at[0])]
    down[0].start()
    for copy in dy_copies[NY - 1:]:
        copy.wait_recv()
    total = dkv_ref[4].astype(F32)
    keep_here = dkv_ref[8].astype(F32)
    for k in range(1, NY):
        first, second = r_ref[0, k - 1].astype(F32), r_ref[1, k - 1].astype(F32)
        total = total + jnp.where(wraps[k], first, second)
        keep_here = keep_here + jnp.where(wraps[k], jnp.zeros_like(first), first)
    zs_ref[0] = total.astype(BF16)
    own_ref[...] = keep_here
    send_plane(1)
    out_move.step(0, 5)
    out_move.step(1, 5)
    for copy in dz_copies:
        copy.wait_recv()
    fin_ref[...] = (own_ref[...] + zr_ref[0].astype(F32) + zr_ref[1].astype(F32)).astype(BF16)
    dkv_copies = []
    for d in range(1, NH):
        to = (head + d) % NH
        rows = pl.ds(pl.multiple_of(to * 32, 32), 32)
        for part, ref in enumerate((gk_ref, gv_ref)):
            copy = remote(fin_ref.at[rows, pl.ds(part * E, E)], ref.at[:, slim],
                          dkv_send.at[part, d], dkv_recv.at[part, d], ctx, to)
            copy.start()
            dkv_copies.append(copy)
    for part, ref in enumerate((gk_ref, gv_ref)):
        copy = pltpu.make_async_copy(fin_ref.at[mine, pl.ds(part * E, E)], ref.at[:, slim],
                                     down_sem.at[1 + part])
        copy.start()
        down.append(copy)
    out_move.finish(0)
    out_move.finish(1)
    for copy in dq_copies + dkv_copies:
        copy.wait_recv()
    for copy in down:
        copy.wait()
    grad_move.drain()
    out_move.drain()
    for copy in q_copies + dq_copies + dkv_copies + dy_copies + dz_copies:
        copy.wait_send()
    for kind in range(2):
        for copy in kv_copies[kind] + z_copies[kind]:
            copy.wait_send()
        for _, _, copy in y_copies[kind]:
            copy.wait_send()


def settle_kernel(*refs):
    for src, dst in zip(refs[:4], refs[4:]):
        dst[...] = src[...]


def on_device(query, key, value, grad_out, doc_ids, relay_mask, drop_bits):
    vm = pl.BlockSpec(memory_space=pltpu.VMEM)
    sm = pl.BlockSpec(memory_space=pltpu.SMEM)
    dma = pltpu.SemaphoreType.DMA
    heads = [dma((2, NH)), dma((2, NH)), dma((NH,)), dma((NH,))]
    up = heads + [dma((2, 3)), dma((2, 3)), dma((2, 2, NY)), dma((2, 2, NY)), dma((3,))]
    down = heads + [dma((3,)), dma((3,)), dma((2, NY)), dma((2, NY)), dma((3,))]
    shapes = (jax.ShapeDtypeStruct((2 * BLK, GROUP * E), BF16),
                   jax.ShapeDtypeStruct((32, NH * GROUP * E), BF16),
                   jax.ShapeDtypeStruct((32, NH * E), BF16),
                   jax.ShapeDtypeStruct((32, NH * E), BF16))
    results = pl.pallas_call(
        whole_kernel,
        out_shape=shapes,
        in_specs=[sm, sm, sm, vm, vm, vm, vm, vm],
        out_specs=(vm, vm, vm, vm),
        scratch_shapes=[
            pltpu.VMEM((2 * BLK, GROUP * E), BF16),
            pltpu.VMEM((9, 2 * BLK, E), BF16),
            pltpu.VMEM((9, 2 * BLK, E), BF16),
            pltpu.VMEM((2 * BLK, GROUP * E), BF16),
            pltpu.VMEM((GROUP, 2 * BLK, BLK), F32),
            pltpu.VMEM((2 * BLK, GROUP * E), BF16),
            pltpu.VMEM((2 * BLK, GROUP * E), BF16),
            pltpu.VMEM((9, 2 * BLK, 2 * E), BF16),
            pltpu.VMEM((2, NY - 1, 2 * BLK, 2 * E), BF16),
            pltpu.VMEM((2, 2 * BLK, 2 * E), BF16),
            pltpu.VMEM((2, 2 * BLK, 2 * E), BF16),
            pltpu.VMEM((2 * BLK, 2 * E), F32),
            pltpu.VMEM((2 * BLK, 2 * E), BF16),
        ] + up + down + relay_scratch() + relay_scratch() + attn_scratch(),
        compiler_params=pltpu.CompilerParams(
            collective_id=0, has_side_effects=True, vmem_limit_bytes=60 * 1024 * 1024),
    )(doc_ids, relay_mask, route_table(), query, key, value, grad_out, drop_bits.transpose(0, 2, 1))
    return pl.pallas_call(
        settle_kernel, out_shape=shapes, in_specs=[vm] * 4, out_specs=(vm,) * 4)(*results)


def solution(mesh):
    placed = (
        P(("ctx", "head"), None),
        P(("ctx", "head"), None),
        P(("ctx", "head"), None),
        P("ctx", "head"),
        P(),
        P(),
        P("head", None, None),
    )
    return jax.shard_map(
        on_device,
        mesh=mesh,
        in_specs=placed,
        out_specs=(
            P("ctx", "head"),
            P(("ctx", "head"), None),
            P(("ctx", "head"), None),
            P(("ctx", "head"), None),
        ),
        check_vma=False,
    )
```
